256 devices in a mesh: space: 32 (over z_lo, x, core), hist: 8 (over z_hi, y).
Axes of the slice: x: 4, y: 4, z: 8 (z_hi: 2, z_lo: 4; z = z_hi * 4 + z_lo), core: 2. Of those that a mesh axis runs over, the one named last changes fastest.
Arguments:
- history: bfloat16 [32, 64, 16384], P('hist', None, 'space'), may hold values from -6 to 6
- right_factor: bfloat16 [512, 80, 16384], P('hist', None, 'space'), may hold values from -0.25 to 0.25
- left_factor: bfloat16 [512, 80, 16384], P('hist', None, 'space'), may hold values from -0.125 to 0.125
- pair_rank: int32 [512, 32], P('hist', 'space'), may hold values from 20 to 80
- pair_lag: int32 [512, 32], P('hist', 'space'), may hold values from 0 to 3
- near_block: bfloat16 [3, 16384, 512], P(None, 'space'), may hold values from -0.09695897 to 0.09695897, as said below
- self_term: float32 [16384], P('space'), may hold values from 1 to 1.5
- excitation: float32 [64, 16384], P(None, 'space'), may hold values from -6 to 6
Outputs:
- new_current: float32 [64, 16384], P(None, 'space')
- next_history: bfloat16 [32, 64, 16384], P('hist', None, 'space')
The draws below stay inside these ranges and needn't reach their ends.
Inputs may be any that keep to these rules, and one draw needn't show every extreme that they name: Entries of near_block lie within 3.8 times (1536) to the power -0.5 in magnitude.
All inputs are finite; a program needn't handle non-finite values.
Results may differ from the reference program's by a relative error of at most 0.015.
Values may be sent and summed in bfloat16 or wider, within the bound.
No kernel may reach another device: no remote copies, remote signals or barrier semaphores. Data moves between devices by JAX's collectives and lax.ppermute only.
A program may use at most 64 MiB of HBM per device.

```python
import jax
import jax.numpy as jnp
from jax import lax

B_DEV = 512
K = 64
RMAX = 80
PPT = 2
LAG_DEV = 4
SWEEPS = 8
N = 16384
PAIR_DEV = 64
NPAIRS = 512
LAGS = 32
N_SPACE = 32
N_HIST = 8


def draw_near_block(key, part):
    spread = 0.95 * (3.0 * B_DEV) ** (-0.5)
    inner = jax.random.fold_in(key, 7301)
    values = jnp.clip(jax.random.normal(inner, (3, N, B_DEV), jnp.float32), -4.0, 4.0) * spread
    values = jnp.clip(values, -3.7 * (3.0 * B_DEV) ** (-0.5), 3.7 * (3.0 * B_DEV) ** (-0.5))
    return values.astype(jnp.bfloat16)


def touch_ends(entries, own_key, low, largest):
    shape = entries.shape
    index_at = [jax.random.randint(jax.random.fold_in(own_key, axis), (), 0, shape[axis]) for axis in range(len(shape))]
    entries = entries.at[tuple(index_at)].set(low)
    longest = shape.index(max(shape))
    index_at[longest] = (index_at[longest] + 1) % shape[longest]
    return entries.at[tuple(index_at)].set(largest)


def block_levels(key, extent, cuts, low, top_value):
    factor_of = 1.0
    for dim, shards_of in cuts:
        steps = jax.random.uniform(jax.random.fold_in(jax.random.fold_in(key, 6), dim), (shards_of,), jnp.float32, low / len(cuts), top_value / len(cuts))
        factor_of = factor_of * jnp.repeat(jnp.exp(steps), extent[dim] // shards_of).reshape((-1,) + (1,) * (len(extent) - 1 - dim))
    return factor_of


def centred(own_key, dims, scale, reach, shards=(), kind=jnp.bfloat16):
    values = jax.random.normal(own_key, dims, jnp.float32) * scale
    if len(shards) > 0:
        values = block_levels(own_key, dims, shards, -0.22, 0.18) * values
    return jnp.clip(values, min=-reach, max=reach).astype(kind)


def setup_inputs(seed: int = 0) -> dict:
    key_list = jax.random.split(jax.random.key(seed), 9)
    history = centred(key_list[0], (LAGS, K, N), 1.0, 6.0, ((0, 8), (2, 32)))
    right_factor = centred(key_list[1], (NPAIRS, RMAX, N), B_DEV ** -0.5, 0.25, ((0, 8), (2, 32)))
    left_factor = centred(key_list[2], (NPAIRS, RMAX, N), (RMAX * PPT * N_HIST * 2) ** -0.5, 0.125, ((0, 8), (2, 32)))
    pair_rank = touch_ends(jax.random.randint(key_list[3], (NPAIRS, N_SPACE), RMAX // 4, RMAX + 1), jax.random.fold_in(key_list[3], 1), RMAX // 4, RMAX).astype(jnp.int32)
    pair_lag = touch_ends(jax.random.randint(key_list[4], (NPAIRS, N_SPACE), 0, LAG_DEV), jax.random.fold_in(key_list[4], 1), 0, LAG_DEV - 1).astype(jnp.int32)
    near_block = draw_near_block(jax.random.fold_in(key_list[8], 71), 0)
    self_term = jnp.clip(1.0 + 0.5 * jax.random.uniform(key_list[6], (N,), jnp.float32) ** block_levels(key_list[6], (N,), ((0, 32),), -0.2, 0.2), 1.0, 1.5)
    excitation = centred(key_list[7], (K, N), 1.0, 6.0, ((1, 32),), jnp.float32)
    return {"history": history, "right_factor": right_factor, "left_factor": left_factor, "pair_rank": pair_rank, "pair_lag": pair_lag, "near_block": near_block, "self_term": self_term, "excitation": excitation}


def reference(history, right_factor, left_factor, pair_rank, pair_lag, near_block, self_term, excitation):
    total = N_SPACE * B_DEV
    pair_count = PAIR_DEV * N_HIST
    group_base = (jnp.arange(pair_count, dtype=jnp.int32) // PAIR_DEV) * LAG_DEV
    levels = jnp.arange(RMAX, dtype=jnp.int32)

    def add_source(source, accum):
        source = jnp.asarray(source).astype(jnp.int32)
        start = (source * B_DEV).astype(jnp.int32)
        right_cols = lax.dynamic_slice_in_dim(right_factor, start, B_DEV, 2)
        left_cols = lax.dynamic_slice_in_dim(left_factor, start, B_DEV, 2)
        hist_cols = lax.dynamic_slice_in_dim(history, start, B_DEV, 2)
        lag_column = lax.dynamic_index_in_dim(pair_lag, source, 1, keepdims=False).astype(jnp.int32)
        ranks = lax.dynamic_index_in_dim(pair_rank, source, 1, keepdims=False)
        chosen = jnp.take(hist_cols, group_base + lag_column, axis=0)
        coefficient = jnp.einsum("prb,pkb->prk", right_cols.astype(jnp.float32), chosen.astype(jnp.float32))
        coefficient = jnp.where(levels[None, :, None] < ranks[:, None, None], coefficient, 0.0).astype(jnp.bfloat16)
        coefficient = coefficient.reshape(N_HIST, N_SPACE, PPT * RMAX, K).astype(jnp.float32)
        left_rows = left_cols.reshape(N_HIST, N_SPACE, PPT * RMAX, B_DEV).astype(jnp.float32)
        return accum + jnp.einsum("htck,htcb->tkb", coefficient, left_rows)

    far_field = lax.fori_loop(0, N_SPACE, add_source, jnp.zeros((N_SPACE, K, B_DEV), jnp.float32))
    far_field = far_field.transpose(1, 0, 2).reshape(K, total)
    right_side = excitation - far_field
    blocks = near_block.astype(jnp.float32).reshape(3, N_SPACE, B_DEV, B_DEV)

    def near_apply(current):
        rounded = lax.optimization_barrier(current.astype(jnp.bfloat16)).astype(jnp.float32)
        padded = jnp.pad(rounded, ((0, 0), (B_DEV, B_DEV)))
        product = self_term[None, :] * current
        for offset in range(3):
            beside = padded[:, offset * B_DEV: offset * B_DEV + total].reshape(K, N_SPACE, B_DEV)
            product = product + jnp.einsum("ktj,tij->kti", beside, blocks[offset]).reshape(K, total)
        return product

    current = jnp.zeros((K, total), jnp.float32)
    for sweep_index in range(SWEEPS):
        current = current + (right_side - near_apply(current)) / self_term[None, :]
    newest = current.astype(jnp.bfloat16)
    next_history = jnp.concatenate([newest[None], history[:-1]], axis=0)
    return current, next_history
```

```python
import functools

import jax
import jax.numpy as jnp
from jax import lax
from jax.experimental import pallas as pl
from jax.experimental.pallas import tpu as pltpu
from jax.sharding import Mesh
from jax.sharding import PartitionSpec as P

SWEEPS = 8
SPACE = ("zl", "x", "c")
HIST = ("zh", "y")


def far_kernel(core_ref, rank_ref, lag_ref, hist_ref, right_ref, left_ref, out_ref, *, ranks):
    group = pl.program_id(0)
    chips, _, depth, width = right_ref.shape
    lags, steps, _ = hist_ref.shape
    total = chips * depth
    lane = lax.broadcasted_iota(jnp.int32, (1, total), 1)
    column = jnp.full((1, total), -1, jnp.int32)
    per = depth // ranks
    for chip in range(chips):
        for k in range(per):
            pair = ((group * chips + chip) * 2 + core_ref[0]) * per + k
            first = (chip * per + k) * ranks
            inside = (lane >= first) & (lane < first + rank_ref[pair])
            column = jnp.where(inside, lag_ref[pair], column)
    right = right_ref[...].reshape(total, width)
    every = lax.dot_general(
        hist_ref[...].reshape(lags * steps, width),
        right,
        (((1,), (1,)), ((), ())),
        preferred_element_type=jnp.float32,
    )
    chosen = jnp.zeros((steps, total), jnp.float32)
    for lag in range(lags):
        chosen = jnp.where(column == lag, every[lag * steps : (lag + 1) * steps], chosen)
    chosen = chosen.astype(jnp.bfloat16)
    left = left_ref[...].reshape(total, width)
    for chip in range(chips):
        first, last = chip * depth, (chip + 1) * depth
        low, high = first // 128 * 128, -(-last // 128) * 128
        part = chosen[:, low:high]
        at = lax.broadcasted_iota(jnp.int32, part.shape, 1) + low
        part = jnp.where((at >= first) & (at < last), part, jnp.zeros_like(part))
        value = jnp.dot(part, left[low:high], preferred_element_type=jnp.float32)
        out_ref[chip] = value.reshape(out_ref.shape[1:]).astype(out_ref.dtype)


def far_half(core, rank, lag, history, right, left, ranks):
    rows, cores, depth, width = right.shape
    lags, steps, _ = history.shape
    groups, chips, cuts = 4, 4, 4
    spec = pl.BlockSpec((chips, 1, depth, width), lambda g, core, *_: (g, core[0], 0, 0))
    return pl.pallas_call(
        functools.partial(far_kernel, ranks=ranks),
        out_shape=jax.ShapeDtypeStruct((chips, cuts, groups, steps // cuts, width), jnp.bfloat16),
        grid_spec=pltpu.PrefetchScalarGridSpec(
            num_scalar_prefetch=3,
            grid=(groups,),
            in_specs=[
                pl.BlockSpec((lags, steps, width), lambda g, *_: (0, 0, 0)),
                spec,
                spec,
            ],
            out_specs=pl.BlockSpec(
                (chips, cuts, 1, steps // cuts, width), lambda g, *_: (0, 0, g, 0, 0)
            ),
        ),
        compiler_params=pltpu.CompilerParams(vmem_limit_bytes=60 * 1024 * 1024),
        cost_estimate=pl.CostEstimate(
            flops=2 * rows * depth * width * (lags + 1) * steps,
            bytes_accessed=rows * depth * width * 4 + rows * steps * width * 2,
            transcendentals=0,
        ),
        name="far_half",
    )(core, rank, lag, history, right, left)


def per_device(
    history, right_factor, left_factor, pair_rank, pair_lag, near_block, self_term, excitation
):
    lags, time_steps, width = history.shape
    pairs, ranks, _ = right_factor.shape
    targets = 32
    depth = pairs // targets * ranks
    right = right_factor.reshape(targets // 2, 2, depth, width)
    left = left_factor.reshape(targets // 2, 2, depth, width)
    rank, lag = pair_rank[:, 0], pair_lag[:, 0]
    core = lax.axis_index("c")
    swap = [(0, 1), (1, 0)]

    def half(which):
        return far_half(which.reshape(1), rank, lag, history, right, left, ranks)

    away = half(1 - core)
    came = lax.ppermute(away, "c", swap)
    mine = half(core)
    partial_value = (mine.astype(jnp.float32) + came.astype(jnp.float32)).astype(jnp.bfloat16)
    arrived = lax.all_to_all(
        partial_value.reshape(16, -1, width), ("x", "y"), 0, 0, tiled=True
    ).reshape(16, 4, -1, width)
    order = [(i, i + 1) for i in range(7)]
    incoming = lax.ppermute(history[-1], HIST, order)
    arrived, incoming = lax.optimization_barrier((arrived, incoming))
    plane = jnp.sum(arrived.astype(jnp.float32), axis=0).astype(jnp.bfloat16)
    twice = jnp.broadcast_to(plane[None], (2, *plane.shape)).reshape(8, -1, width)
    arrived = lax.all_to_all(twice, ("zh", "zl"), 0, 0, tiled=True)
    far_field = jnp.sum(arrived.astype(jnp.float32), axis=0)
    rows = time_steps // 4
    cut = lax.axis_index("y") * rows
    right_side = lax.dynamic_slice_in_dim(excitation, cut, rows, 0) - far_field

    inverse = 1.0 / self_term[None, :]
    near_own = near_block[1]
    near_chip = jnp.where(core == 0, near_block[2], near_block[0])
    near_away = jnp.where(core == 0, near_block[0], near_block[2])
    between = []
    for t in range(1, targets - 1, 2):
        between += [(t, t + 1), (t + 1, t)]

    def product(value, block):
        return lax.dot_general(
            value, block, (((1,), (1,)), ((), ())), preferred_element_type=jnp.float32
        )

    current = right_side * inverse
    for _ in range(SWEEPS - 1):
        rounded = current.astype(jnp.bfloat16)
        far = lax.ppermute(rounded, SPACE, between)
        chip = lax.ppermute(rounded, "c", swap)
        total = product(rounded, near_own) + product(chip, near_chip)
        total = total + product(far, near_away)
        current = (right_side - total) * inverse

    everywhere = lax.all_to_all(
        jnp.broadcast_to(current[None], (4, *current.shape)), "y", 0, 0, tiled=True
    ).reshape(time_steps, width)
    oldest = (lax.axis_index("zh") == 0) & (lax.axis_index("y") == 0)
    newest = jnp.where(oldest, everywhere.astype(jnp.bfloat16), incoming)
    next_history = jnp.concatenate([newest[None], history[:-1]], axis=0)
    return (everywhere, next_history)


def solution(mesh):
    fine = Mesh(mesh.devices.reshape(4, 4, 2, 2, 4), SPACE + HIST)
    in_specs = (
        P(HIST, None, SPACE),
        P(HIST, None, SPACE),
        P(HIST, None, SPACE),
        P(HIST, SPACE),
        P(HIST, SPACE),
        P(None, SPACE, None),
        P(SPACE),
        P(None, SPACE),
    )
    out_specs = (P(None, SPACE), P(HIST, None, SPACE))
    return jax.shard_map(
        per_device, mesh=fine, in_specs=in_specs, out_specs=out_specs, check_vma=False
    )
```

```python
import functools

import jax
import jax.numpy as jnp
from jax import lax
from jax.experimental import pallas as pl
from jax.experimental.pallas import tpu as pltpu
from jax.sharding import Mesh
from jax.sharding import PartitionSpec as P


SWEEPS = 8
SPACE = ("zl", "x", "c")
HIST = ("zh", "y")


def far_kernel(
    core_ref, rank_ref, lag_ref, hist_ref, right_ref, left_ref, out_ref,
    hist_buf, right_buf, left_buf, hist_sem, right_sem, left_sem, *, ranks
):
    groups, chips, depth, width = right_buf.shape
    lags, steps, _ = hist_buf.shape
    total = chips * depth
    core = core_ref[0]

    def brought(source, target, sem, group):
        return pltpu.make_async_copy(
            source.at[pl.ds(group * chips, chips), core], target.at[group], sem.at[group]
        )

    whole = pltpu.make_async_copy(hist_ref, hist_buf, hist_sem)
    whole.start()
    rights = [brought(right_ref, right_buf, right_sem, g) for g in range(groups)]
    lefts = [brought(left_ref, left_buf, left_sem, g) for g in range(groups)]
    for g in range(groups):
        rights[g].start()
        lefts[g].start()
    lane = lax.broadcasted_iota(jnp.int32, (1, total), 1)
    per = depth // ranks

    def chosen(group):
        column = jnp.full((1, total), -1, jnp.int32)
        for chip in range(chips):
            for k in range(per):
                pair = ((group * chips + chip) * 2 + core) * per + k
                first = (chip * per + k) * ranks
                inside = (lane >= first) & (lane < first + rank_ref[pair])
                column = jnp.where(inside, lag_ref[pair], column)
        every = lax.dot_general(
            hist_buf[...].reshape(lags * steps, width),
            right_buf[group].reshape(total, width),
            (((1,), (1,)), ((), ())),
            preferred_element_type=jnp.float32,
        )
        value = jnp.zeros((steps, total), jnp.float32)
        for lag in range(lags):
            value = jnp.where(column == lag, every[lag * steps : (lag + 1) * steps], value)
        return value.astype(jnp.bfloat16)

    def far(group, value):
        left = left_buf[group].reshape(total, width)
        for chip in range(chips):
            first, last = chip * depth, (chip + 1) * depth
            low, high = first // 128 * 128, -(-last // 128) * 128
            part = value[:, low:high]
            at = lax.broadcasted_iota(jnp.int32, part.shape, 1) + low
            part = jnp.where((at >= first) & (at < last), part, jnp.zeros_like(part))
            field = jnp.dot(part, left[low:high], preferred_element_type=jnp.float32)
            out_ref[chip, :, group] = field.reshape(out_ref.shape[1], -1, width).astype(out_ref.dtype)

    whole.wait()
    rights[0].wait()
    value = chosen(0)
    for g in range(groups):
        lefts[g].wait()
        ahead = None
        if g + 1 < groups:
            rights[g + 1].wait()
            ahead = chosen(g + 1)
        far(g, value)
        value = ahead


def far_half(core, rank, lag, history, right, left, ranks):
    rows, _, depth, width = right.shape
    lags, steps, _ = history.shape
    groups, chips, cuts = 4, 4, 4
    scalar = pl.BlockSpec(memory_space=pltpu.SMEM)
    outside = pl.BlockSpec(memory_space=pltpu.HBM)
    held = pltpu.VMEM((groups, chips, depth, width), jnp.bfloat16)
    return pl.pallas_call(
        functools.partial(far_kernel, ranks=ranks),
        out_shape=jax.ShapeDtypeStruct((chips, cuts, groups, steps // cuts, width), jnp.bfloat16),
        in_specs=[scalar, scalar, scalar, outside, outside, outside],
        out_specs=pl.BlockSpec(memory_space=pltpu.VMEM),
        scratch_shapes=[
            pltpu.VMEM((lags, steps, width), jnp.bfloat16),
            held,
            held,
            pltpu.SemaphoreType.DMA,
            pltpu.SemaphoreType.DMA((groups,)),
            pltpu.SemaphoreType.DMA((groups,)),
        ],
        compiler_params=pltpu.CompilerParams(vmem_limit_bytes=16 << 20),
        cost_estimate=pl.CostEstimate(
            flops=2 * rows * depth * width * (lags + 1) * steps,
            bytes_accessed=rows * depth * width * 4 + rows * steps * width * 2,
            transcendentals=0,
        ),
        name="far_half",
    )(core, rank, lag, history, right, left)


def per_device(
    history, right_factor, left_factor, pair_rank, pair_lag, near_block, self_term, excitation
):
    _, time_steps, width = history.shape
    pairs, ranks, _ = right_factor.shape
    targets = 32
    depth = pairs // targets * ranks
    right = right_factor.reshape(targets // 2, 2, depth, width)
    left = left_factor.reshape(targets // 2, 2, depth, width)
    rank, lag = pair_rank[:, 0], pair_lag[:, 0]
    history_out, right, left = (
        pltpu.with_memory_space_constraint(v, pltpu.HBM) for v in (history, right, left)
    )
    core = lax.axis_index("c")
    swap = [(0, 1), (1, 0)]

    def half(which):
        return far_half(which.reshape(1), rank, lag, history_out, right, left, ranks)

    away = half(1 - core)
    came = lax.ppermute(away, "c", swap)
    mine = half(core)
    partial_value = (mine.astype(jnp.float32) + came.astype(jnp.float32)).astype(jnp.bfloat16)
    arrived = lax.all_to_all(
        partial_value.reshape(16, -1, width), ("x", "y"), 0, 0, tiled=True
    ).reshape(16, 4, -1, width)
    plane = jnp.sum(arrived.astype(jnp.float32), axis=0).astype(jnp.bfloat16)
    twice = jnp.broadcast_to(plane[None], (2, *plane.shape)).reshape(8, -1, width)
    arrived = lax.all_to_all(twice, ("zh", "zl"), 0, 0, tiled=True)
    incoming = lax.ppermute(history[-1], HIST, [(i, i + 1) for i in range(7)])
    shifted = jnp.concatenate([incoming[None], history[:-1]], axis=0)
    arrived, incoming, shifted = lax.optimization_barrier((arrived, incoming, shifted))
    far_field = jnp.sum(arrived.astype(jnp.float32), axis=0)
    rows = time_steps // 4
    row = lax.axis_index("y")
    right_side = lax.dynamic_slice_in_dim(excitation, row * rows, rows, 0) - far_field

    inverse = 1.0 / self_term[None, :]
    near_own = near_block[1]
    near_chip = jnp.where(core == 0, near_block[2], near_block[0])
    near_away = jnp.where(core == 0, near_block[0], near_block[2])
    between = []
    for t in range(1, targets - 1, 2):
        between += [(t, t + 1), (t + 1, t)]

    def product(value, block):
        return lax.dot_general(
            value, block, (((1,), (1,)), ((), ())), preferred_element_type=jnp.float32
        )

    current = right_side * inverse
    for _ in range(1, SWEEPS):
        rounded = current.astype(jnp.bfloat16)
        away = lax.ppermute(rounded, SPACE, between)
        chip = lax.ppermute(rounded, "c", swap)
        total = product(rounded, near_own)
        total = total + product(chip, near_chip)
        total = total + product(away, near_away)
        current = (right_side - total) * inverse

    pieces = [current]
    for step in (2, 1, 3):
        pieces.append(
            lax.ppermute(current, "y", [(i, (i + step) % 4) for i in range(4)])
        )
    everywhere = []
    for slot in range(4):
        value = pieces[0]
        for step, piece in zip((2, 1, 3), pieces[1:]):
            value = jnp.where(row == (slot + step) % 4, piece, value)
        everywhere.append(value)
    everywhere = jnp.concatenate(everywhere, axis=0)
    oldest = (lax.axis_index("zh") == 0) & (row == 0)
    newest = jnp.where(oldest, everywhere.astype(jnp.bfloat16), incoming)
    next_history = lax.dynamic_update_slice_in_dim(shifted, newest[None], 0, 0)
    return (everywhere, next_history)


def solution(mesh):
    fine = Mesh(mesh.devices.reshape(4, 4, 2, 2, 4), SPACE + HIST)
    in_specs = (
        P(HIST, None, SPACE),
        P(HIST, None, SPACE),
        P(HIST, None, SPACE),
        P(HIST, SPACE),
        P(HIST, SPACE),
        P(None, SPACE, None),
        P(SPACE),
        P(None, SPACE),
    )
    out_specs = (P(None, SPACE), P(HIST, None, SPACE))
    return jax.shard_map(
        per_device, mesh=fine, in_specs=in_specs, out_specs=out_specs, check_vma=False
    )
```

```python
import functools

import jax
import jax.numpy as jnp
from jax import lax
from jax.experimental import pallas as pl
from jax.experimental.pallas import tpu as pltpu
from jax.sharding import Mesh
from jax.sharding import PartitionSpec as P


SWEEPS = 8
SPACE = ("zl", "x", "c")
HIST = ("zh", "y")


def far_kernel(
    core_ref, rank_ref, lag_ref, hist_ref, right_ref, left_ref, out_ref,
    rank_buf, lag_buf, hist_buf, right_buf, left_buf,
    rank_sem, lag_sem, hist_sem, right_sem, left_sem, *, ranks
):
    groups, chips, depth, width = right_buf.shape
    lags, steps, _ = hist_buf.shape
    total = chips * depth
    core = core_ref[0]

    def brought(source, target, sem, group):
        return pltpu.make_async_copy(
            source.at[pl.ds(group * chips, chips), core], target.at[group], sem.at[group]
        )

    small = [
        pltpu.make_async_copy(rank_ref, rank_buf, rank_sem),
        pltpu.make_async_copy(lag_ref, lag_buf, lag_sem),
        pltpu.make_async_copy(hist_ref, hist_buf, hist_sem),
    ]
    for copy in small:
        copy.start()
    rights = [brought(right_ref, right_buf, right_sem, g) for g in range(groups)]
    lefts = [brought(left_ref, left_buf, left_sem, g) for g in range(groups)]
    for g in range(groups):
        rights[g].start()
        lefts[g].start()
    lane = lax.broadcasted_iota(jnp.int32, (1, total), 1)
    per = depth // ranks

    def chosen(group):
        column = jnp.full((1, total), -1, jnp.int32)
        for chip in range(chips):
            for k in range(per):
                pair = ((group * chips + chip) * 2 + core) * per + k
                first = (chip * per + k) * ranks
                inside = (lane >= first) & (lane < first + rank_buf[pair])
                column = jnp.where(inside, lag_buf[pair], column)
        every = lax.dot_general(
            hist_buf[...].reshape(lags * steps, width),
            right_buf[group].reshape(total, width),
            (((1,), (1,)), ((), ())),
            preferred_element_type=jnp.float32,
        )
        value = jnp.zeros((steps, total), jnp.float32)
        for lag in range(lags):
            value = jnp.where(column == lag, every[lag * steps : (lag + 1) * steps], value)
        return value.astype(jnp.bfloat16)

    def far(group, value):
        left = left_buf[group].reshape(total, width)
        for chip in range(chips):
            first, last = chip * depth, (chip + 1) * depth
            low, high = first // 128 * 128, -(-last // 128) * 128
            part = value[:, low:high]
            at = lax.broadcasted_iota(jnp.int32, part.shape, 1) + low
            part = jnp.where((at >= first) & (at < last), part, jnp.zeros_like(part))
            field = jnp.dot(part, left[low:high], preferred_element_type=jnp.float32)
            out_ref[chip, :, group] = field.reshape(out_ref.shape[1], -1, width).astype(out_ref.dtype)

    for copy in small:
        copy.wait()
    rights[0].wait()
    value = chosen(0)
    for g in range(groups):
        lefts[g].wait()
        ahead = None
        if g + 1 < groups:
            rights[g + 1].wait()
            ahead = chosen(g + 1)
        far(g, value)
        value = ahead


def far_half(core, rank, lag, history, right, left, ranks):
    rows, _, depth, width = right.shape
    lags, steps, _ = history.shape
    groups, chips, cuts = 4, 4, 4
    scalar = pl.BlockSpec(memory_space=pltpu.SMEM)
    outside = pl.BlockSpec(memory_space=pltpu.HBM)
    held = pltpu.VMEM((groups, chips, depth, width), jnp.bfloat16)
    return pl.pallas_call(
        functools.partial(far_kernel, ranks=ranks),
        out_shape=jax.ShapeDtypeStruct((chips, cuts, groups, steps // cuts, width), jnp.bfloat16),
        in_specs=[scalar] + [outside] * 5,
        out_specs=pl.BlockSpec(memory_space=pltpu.VMEM),
        scratch_shapes=[
            pltpu.SMEM(rank.shape, jnp.int32),
            pltpu.SMEM(lag.shape, jnp.int32),
            pltpu.VMEM((lags, steps, width), jnp.bfloat16),
            held,
            held,
            pltpu.SemaphoreType.DMA,
            pltpu.SemaphoreType.DMA,
            pltpu.SemaphoreType.DMA,
            pltpu.SemaphoreType.DMA((groups,)),
            pltpu.SemaphoreType.DMA((groups,)),
        ],
        compiler_params=pltpu.CompilerParams(vmem_limit_bytes=16 << 20),
        cost_estimate=pl.CostEstimate(
            flops=2 * rows * depth * width * (lags + 1) * steps,
            bytes_accessed=rows * depth * width * 4 + rows * steps * width * 2,
            transcendentals=0,
        ),
        name="far_half",
    )(core, rank, lag, history, right, left)


def plane_kernel(in_ref, out_ref):
    rows = 16
    for first in range(0, in_ref.shape[1], rows):
        part = slice(first, first + rows)
        total = in_ref[0, part].astype(jnp.float32)
        for source in range(1, in_ref.shape[0]):
            total = total + in_ref[source, part].astype(jnp.float32)
        for copy in range(out_ref.shape[0]):
            out_ref[copy, part] = total.astype(out_ref.dtype)


def plane_sum(arrived, copies):
    inside = pl.BlockSpec(memory_space=pltpu.VMEM)
    return pl.pallas_call(
        plane_kernel,
        out_shape=jax.ShapeDtypeStruct((copies, *arrived.shape[1:]), arrived.dtype),
        in_specs=[inside],
        out_specs=inside,
        compiler_params=pltpu.CompilerParams(vmem_limit_bytes=4 << 20),
        cost_estimate=pl.CostEstimate(
            flops=arrived.size, bytes_accessed=2 * arrived.size, transcendentals=0
        ),
        name="plane_sum",
    )(arrived)


def per_device(
    history, right_factor, left_factor, pair_rank, pair_lag, near_block, self_term, excitation
):
    _, time_steps, width = history.shape
    pairs, ranks, _ = right_factor.shape
    targets = 32
    depth = pairs // targets * ranks
    right = right_factor.reshape(targets // 2, 2, depth, width)
    left = left_factor.reshape(targets // 2, 2, depth, width)
    history_out, right, left, rank, lag = (
        pltpu.with_memory_space_constraint(v, pltpu.HBM)
        for v in (history, right, left, pair_rank[:, 0], pair_lag[:, 0])
    )
    core = lax.axis_index("c")
    swap = [(0, 1), (1, 0)]

    def half(which):
        return far_half(which.reshape(1), rank, lag, history_out, right, left, ranks)

    away = half(1 - core)
    came = lax.ppermute(away, "c", swap)
    mine = half(core)
    partial_value = (mine.astype(jnp.float32) + came.astype(jnp.float32)).astype(jnp.bfloat16)
    arrived = lax.all_to_all(
        partial_value.reshape(16, -1, width), ("x", "y"), 0, 0, tiled=True
    )
    twice = plane_sum(arrived, 2).reshape(8, -1, width)
    arrived = lax.all_to_all(twice, ("zh", "zl"), 0, 0, tiled=True)
    incoming = lax.ppermute(history[-1], HIST, [(i, (i + 1) % 8) for i in range(8)])
    shifted = jnp.concatenate([incoming[None], history[:-1]], axis=0)
    arrived, incoming, shifted = lax.optimization_barrier((arrived, incoming, shifted))
    far_field = jnp.sum(arrived.astype(jnp.float32), axis=0)
    rows = time_steps // 4
    row = lax.axis_index("y")
    right_side = lax.dynamic_slice_in_dim(excitation, row * rows, rows, 0) - far_field

    inverse = 1.0 / self_term[None, :]
    near_own = near_block[1]
    near_chip = jnp.where(core == 0, near_block[2], near_block[0])
    near_away = jnp.where(core == 0, near_block[0], near_block[2])
    block = lax.axis_index(SPACE)
    near_away = jnp.where((block == 0) | (block == targets - 1), 0.0, near_away)
    between = [(0, 0), (targets - 1, targets - 1)]
    for t in range(1, targets - 1, 2):
        between += [(t, t + 1), (t + 1, t)]

    def product(value, block):
        return lax.dot_general(
            value, block, (((1,), (1,)), ((), ())), preferred_element_type=jnp.float32
        )

    current = right_side * inverse
    for _ in range(1, SWEEPS):
        rounded = current.astype(jnp.bfloat16)
        away = lax.ppermute(rounded, SPACE, between)
        chip = lax.ppermute(rounded, "c", swap)
        total = product(rounded, near_own)
        total = total + product(chip, near_chip)
        total = total + product(away, near_away)
        current = (right_side - total) * inverse

    pieces = [current]
    for step in (2, 1, 3):
        pieces.append(
            lax.ppermute(current, "y", [(i, (i + step) % 4) for i in range(4)])
        )
    everywhere = []
    for slot in range(4):
        value = pieces[0]
        for step, piece in zip((2, 1, 3), pieces[1:]):
            value = jnp.where(row == (slot + step) % 4, piece, value)
        everywhere.append(value)
    everywhere = jnp.concatenate(everywhere, axis=0)
    oldest = (lax.axis_index("zh") == 0) & (row == 0)
    newest = jnp.where(oldest, everywhere.astype(jnp.bfloat16), incoming)
    next_history = lax.dynamic_update_slice_in_dim(shifted, newest[None], 0, 0)
    return (everywhere, next_history)


def solution(mesh):
    fine = Mesh(mesh.devices.reshape(4, 4, 2, 2, 4), SPACE + HIST)
    in_specs = (
        P(HIST, None, SPACE),
        P(HIST, None, SPACE),
        P(HIST, None, SPACE),
        P(HIST, SPACE),
        P(HIST, SPACE),
        P(None, SPACE, None),
        P(SPACE),
        P(None, SPACE),
    )
    out_specs = (P(None, SPACE), P(HIST, None, SPACE))
    return jax.shard_map(
        per_device, mesh=fine, in_specs=in_specs, out_specs=out_specs, check_vma=False
    )
```

```python
import functools

import jax
import jax.numpy as jnp
from jax import lax
from jax.experimental import pallas as pl
from jax.experimental.pallas import tpu as pltpu
from jax.sharding import Mesh
from jax.sharding import PartitionSpec as P


SWEEPS = 8
SPACE = ("zl", "x", "c")
HIST = ("zh", "y")


def far_kernel(
    core_ref, rank_ref, lag_ref, hist_ref, right_ref, left_ref, out_ref,
    rank_buf, lag_buf, hist_buf, right_buf, left_buf,
    rank_sem, lag_sem, hist_sem, right_sem, left_sem, *, ranks
):
    groups, chips, depth, width = right_buf.shape
    lags, steps, _ = hist_buf.shape
    total = chips * depth
    core = core_ref[0]

    def brought(source, target, sem, group):
        return pltpu.make_async_copy(
            source.at[pl.ds(group * chips, chips), core], target.at[group], sem.at[group]
        )

    small = [
        pltpu.make_async_copy(rank_ref, rank_buf, rank_sem),
        pltpu.make_async_copy(lag_ref, lag_buf, lag_sem),
        pltpu.make_async_copy(hist_ref, hist_buf, hist_sem),
    ]
    for copy in small:
        copy.start()
    rights = [brought(right_ref, right_buf, right_sem, g) for g in range(groups)]
    lefts = [brought(left_ref, left_buf, left_sem, g) for g in range(groups)]
    for g in range(groups):
        rights[g].start()
        lefts[g].start()
    lane = lax.broadcasted_iota(jnp.int32, (1, total), 1)
    per = depth // ranks

    def chosen(group):
        column = jnp.full((1, total), -1, jnp.int32)
        for chip in range(chips):
            for k in range(per):
                pair = ((group * chips + chip) * 2 + core) * per + k
                first = (chip * per + k) * ranks
                inside = (lane >= first) & (lane < first + rank_buf[pair])
                column = jnp.where(inside, lag_buf[pair], column)
        every = lax.dot_general(
            hist_buf[...].reshape(lags * steps, width),
            right_buf[group].reshape(total, width),
            (((1,), (1,)), ((), ())),
            preferred_element_type=jnp.float32,
        )
        value = jnp.zeros((steps, total), jnp.float32)
        for lag in range(lags):
            value = jnp.where(column == lag, every[lag * steps : (lag + 1) * steps], value)
        return value.astype(jnp.bfloat16)

    def far(group, value):
        left = left_buf[group].reshape(total, width)
        for chip in range(chips):
            first, last = chip * depth, (chip + 1) * depth
            low, high = first // 128 * 128, -(-last // 128) * 128
            part = value[:, low:high]
            at = lax.broadcasted_iota(jnp.int32, part.shape, 1) + low
            part = jnp.where((at >= first) & (at < last), part, jnp.zeros_like(part))
            field = jnp.dot(part, left[low:high], preferred_element_type=jnp.float32)
            out_ref[chip, :, group] = field.reshape(out_ref.shape[1], -1, width).astype(out_ref.dtype)

    for copy in small:
        copy.wait()
    rights[0].wait()
    value = chosen(0)
    for g in range(groups):
        lefts[g].wait()
        ahead = None
        if g + 1 < groups:
            rights[g + 1].wait()
            ahead = chosen(g + 1)
        far(g, value)
        value = ahead


def far_half(core, rank, lag, history, right, left, ranks):
    rows, _, depth, width = right.shape
    lags, steps, _ = history.shape
    groups, chips, cuts = 4, 4, 4
    scalar = pl.BlockSpec(memory_space=pltpu.SMEM)
    outside = pl.BlockSpec(memory_space=pltpu.HBM)
    held = pltpu.VMEM((groups, chips, depth, width), jnp.bfloat16)
    return pl.pallas_call(
        functools.partial(far_kernel, ranks=ranks),
        out_shape=jax.ShapeDtypeStruct((chips, cuts, groups, steps // cuts, width), jnp.bfloat16),
        in_specs=[scalar] + [outside] * 5,
        out_specs=pl.BlockSpec(memory_space=pltpu.VMEM),
        scratch_shapes=[
            pltpu.SMEM(rank.shape, jnp.int32),
            pltpu.SMEM(lag.shape, jnp.int32),
            pltpu.VMEM((lags, steps, width), jnp.bfloat16),
            held,
            held,
            pltpu.SemaphoreType.DMA,
            pltpu.SemaphoreType.DMA,
            pltpu.SemaphoreType.DMA,
            pltpu.SemaphoreType.DMA((groups,)),
            pltpu.SemaphoreType.DMA((groups,)),
        ],
        compiler_params=pltpu.CompilerParams(vmem_limit_bytes=16 << 20),
        cost_estimate=pl.CostEstimate(
            flops=2 * rows * depth * width * (lags + 1) * steps,
            bytes_accessed=rows * depth * width * 4 + rows * steps * width * 2,
            transcendentals=0,
        ),
        name="far_half",
    )(core, rank, lag, history, right, left)


def plane_kernel(in_ref, out_ref):
    rows = 16
    for first in range(0, in_ref.shape[1], rows):
        part = slice(first, first + rows)
        total = in_ref[0, part].astype(jnp.float32)
        for source in range(1, in_ref.shape[0]):
            total = total + in_ref[source, part].astype(jnp.float32)
        for copy in range(out_ref.shape[0]):
            out_ref[copy, part] = total.astype(out_ref.dtype)


def plane_sum(arrived, copies):
    inside = pl.BlockSpec(memory_space=pltpu.VMEM)
    return pl.pallas_call(
        plane_kernel,
        out_shape=jax.ShapeDtypeStruct((copies, *arrived.shape[1:]), arrived.dtype),
        in_specs=[inside],
        out_specs=inside,
        compiler_params=pltpu.CompilerParams(vmem_limit_bytes=4 << 20),
        cost_estimate=pl.CostEstimate(
            flops=arrived.size, bytes_accessed=2 * arrived.size, transcendentals=0
        ),
        name="plane_sum",
    )(arrived)


def last_kernel(
    where_ref, own_ref, second_ref, first_ref, third_ref, incoming_ref, shifted_ref,
    out_ref, next_ref, whole_ref, front_ref, out_sem, next_sem
):
    row = where_ref[0]
    rows = own_ref.shape[0]
    for turn, piece in enumerate((own_ref, first_ref, second_ref, third_ref)):
        slot = lax.rem(row + 4 - turn, 4)
        at = pl.ds(pl.multiple_of(slot * rows, rows), rows)
        whole_ref[at] = piece[...]
        front_ref[at] = piece[...].astype(front_ref.dtype)
    whole = pltpu.make_async_copy(whole_ref, out_ref, out_sem)
    whole.start()
    front_ref[...] = jnp.where(where_ref[1] == 1, front_ref[...], incoming_ref[...])
    front = pltpu.make_async_copy(front_ref, next_ref.at[0], next_sem)
    front.start()
    whole.wait()
    front.wait()


def finish(where, pieces, incoming, shifted):
    steps, width = incoming.shape
    inside, outside = (pl.BlockSpec(memory_space=m) for m in (pltpu.VMEM, pltpu.HBM))
    return pl.pallas_call(
        last_kernel,
        out_shape=(
            jax.ShapeDtypeStruct((steps, width), jnp.float32),
            jax.ShapeDtypeStruct(shifted.shape, shifted.dtype),
        ),
        in_specs=[pl.BlockSpec(memory_space=pltpu.SMEM)] + [inside] * 5 + [outside],
        out_specs=(outside, outside),
        scratch_shapes=[
            pltpu.VMEM((steps, width), jnp.float32),
            pltpu.VMEM((steps, width), jnp.bfloat16),
            pltpu.SemaphoreType.DMA,
            pltpu.SemaphoreType.DMA,
        ],
        input_output_aliases={6: 1},
        compiler_params=pltpu.CompilerParams(vmem_limit_bytes=4 << 20),
        name="finish",
    )(where, *pieces, incoming, shifted)


def per_device(
    history, right_factor, left_factor, pair_rank, pair_lag, near_block, self_term, excitation
):
    _, time_steps, width = history.shape
    pairs, ranks, _ = right_factor.shape
    targets = 32
    depth = pairs // targets * ranks
    right = right_factor.reshape(targets // 2, 2, depth, width)
    left = left_factor.reshape(targets // 2, 2, depth, width)
    history_out, right, left, rank, lag = (
        pltpu.with_memory_space_constraint(v, pltpu.HBM)
        for v in (history, right, left, pair_rank[:, 0], pair_lag[:, 0])
    )
    core = lax.axis_index("c")
    swap = [(0, 1), (1, 0)]

    def half(which):
        return far_half(which.reshape(1), rank, lag, history_out, right, left, ranks)

    away = half(1 - core)
    came = lax.ppermute(away, "c", swap)
    mine = half(core)
    partial_value = (mine.astype(jnp.float32) + came.astype(jnp.float32)).astype(jnp.bfloat16)
    arrived = lax.all_to_all(
        partial_value.reshape(16, -1, width), ("x", "y"), 0, 0, tiled=True
    )
    twice = plane_sum(arrived, 2).reshape(8, -1, width)
    arrived = lax.all_to_all(twice, ("zh", "zl"), 0, 0, tiled=True)
    incoming = lax.ppermute(history[-1], HIST, [(i, (i + 1) % 8) for i in range(8)])
    shifted = jnp.concatenate([incoming[None], history[:-1]], axis=0)
    arrived, incoming, shifted = lax.optimization_barrier((arrived, incoming, shifted))
    far_field = jnp.sum(arrived.astype(jnp.float32), axis=0)
    rows = time_steps // 4
    row = lax.axis_index("y")
    right_side = lax.dynamic_slice_in_dim(excitation, row * rows, rows, 0) - far_field

    inverse = 1.0 / self_term[None, :]
    near_own = near_block[1]
    near_chip = jnp.where(core == 0, near_block[2], near_block[0])
    near_away = jnp.where(core == 0, near_block[0], near_block[2])
    block = lax.axis_index(SPACE)
    near_away = jnp.where((block == 0) | (block == targets - 1), 0.0, near_away)
    partner = {0: 0, targets - 1: targets - 1}
    for t in range(1, targets - 1, 2):
        partner[t], partner[t + 1] = t + 1, t
    between = []
    for t, other in partner.items():
        for y in range(4):
            between.append((t * 4 + y, other * 4 + (y ^ 1 if other == t else y)))

    def product(value, block):
        return lax.dot_general(
            value, block, (((1,), (1,)), ((), ())), preferred_element_type=jnp.float32
        )

    current = right_side * inverse
    for _ in range(1, SWEEPS):
        rounded = current.astype(jnp.bfloat16)
        away = lax.ppermute(rounded, SPACE + ("y",), between)
        chip = lax.ppermute(rounded, "c", swap)
        total = product(rounded, near_own)
        total = total + product(chip, near_chip)
        total = total + product(away, near_away)
        current = (right_side - total) * inverse

    pieces = [current]
    for step in (2, 1, 3):
        pieces.append(
            lax.ppermute(current, "y", [(i, (i + step) % 4) for i in range(4)])
        )
    oldest = ((lax.axis_index("zh") == 0) & (row == 0)).astype(jnp.int32)
    return finish(jnp.stack([row, oldest]), pieces, incoming, shifted)


def solution(mesh):
    fine = Mesh(mesh.devices.reshape(4, 4, 2, 2, 4), SPACE + HIST)
    in_specs = (
        P(HIST, None, SPACE),
        P(HIST, None, SPACE),
        P(HIST, None, SPACE),
        P(HIST, SPACE),
        P(HIST, SPACE),
        P(None, SPACE, None),
        P(SPACE),
        P(None, SPACE),
    )
    out_specs = (P(None, SPACE), P(HIST, None, SPACE))
    return jax.shard_map(
        per_device, mesh=fine, in_specs=in_specs, out_specs=out_specs, check_vma=False
    )
```

```python
import functools

import jax
import jax.numpy as jnp
from jax import lax
from jax.experimental import pallas as pl
from jax.experimental.pallas import tpu as pltpu
from jax.sharding import Mesh
from jax.sharding import PartitionSpec as P


SWEEPS = 8
SPACE = ("zl", "x", "c")
HIST = ("zh", "y")


def far_kernel(
    core_ref, rank_ref, lag_ref, hist_ref, right_ref, left_ref, out_ref,
    rank_buf, lag_buf, hist_buf, right_buf, left_buf,
    rank_sem, lag_sem, hist_sem, right_sem, left_sem, *, ranks
):
    groups, chips, depth, width = right_buf.shape
    lags, steps, _ = hist_buf.shape
    total = chips * depth
    core = core_ref[0]

    def brought(source, target, sem, group):
        return pltpu.make_async_copy(
            source.at[pl.ds(group * chips, chips), core], target.at[group], sem.at[group]
        )

    small = [
        pltpu.make_async_copy(rank_ref, rank_buf, rank_sem),
        pltpu.make_async_copy(lag_ref, lag_buf, lag_sem),
        pltpu.make_async_copy(hist_ref, hist_buf, hist_sem),
    ]
    for copy in small:
        copy.start()
    rights = [brought(right_ref, right_buf, right_sem, g) for g in range(groups)]
    lefts = [brought(left_ref, left_buf, left_sem, g) for g in range(groups)]
    for g in range(groups):
        rights[g].start()
        lefts[g].start()
    lane = lax.broadcasted_iota(jnp.int32, (1, total), 1)
    per = depth // ranks

    def chosen(group):
        column = jnp.full((1, total), -1, jnp.int32)
        for chip in range(chips):
            for k in range(per):
                pair = ((group * chips + chip) * 2 + core) * per + k
                first = (chip * per + k) * ranks
                inside = (lane >= first) & (lane < first + rank_buf[pair])
                column = jnp.where(inside, lag_buf[pair], column)
        every = lax.dot_general(
            hist_buf[...].reshape(lags * steps, width),
            right_buf[group].reshape(total, width),
            (((1,), (1,)), ((), ())),
            preferred_element_type=jnp.float32,
        )
        value = jnp.zeros((steps, total), jnp.float32)
        for lag in range(lags):
            value = jnp.where(column == lag, every[lag * steps : (lag + 1) * steps], value)
        return value.astype(jnp.bfloat16)

    def far(group, value):
        left = left_buf[group].reshape(total, width)
        for chip in range(chips):
            first, last = chip * depth, (chip + 1) * depth
            low, high = first // 128 * 128, -(-last // 128) * 128
            part = value[:, low:high]
            at = lax.broadcasted_iota(jnp.int32, part.shape, 1) + low
            part = jnp.where((at >= first) & (at < last), part, jnp.zeros_like(part))
            field = jnp.dot(part, left[low:high], preferred_element_type=jnp.float32)
            out_ref[chip, :, group] = field.reshape(out_ref.shape[1], -1, width).astype(out_ref.dtype)

    for copy in small:
        copy.wait()
    rights[0].wait()
    value = chosen(0)
    for g in range(groups):
        lefts[g].wait()
        ahead = None
        if g + 1 < groups:
            rights[g + 1].wait()
            ahead = chosen(g + 1)
        far(g, value)
        value = ahead


def far_half(core, rank, lag, history, right, left, ranks):
    rows, _, depth, width = right.shape
    lags, steps, _ = history.shape
    groups, chips, cuts = 4, 4, 4
    scalar = pl.BlockSpec(memory_space=pltpu.SMEM)
    outside = pl.BlockSpec(memory_space=pltpu.HBM)
    held = pltpu.VMEM((groups, chips, depth, width), jnp.bfloat16)
    return pl.pallas_call(
        functools.partial(far_kernel, ranks=ranks),
        out_shape=jax.ShapeDtypeStruct((chips, cuts, groups, steps // cuts, width), jnp.bfloat16),
        in_specs=[scalar] + [outside] * 5,
        out_specs=pl.BlockSpec(memory_space=pltpu.VMEM),
        scratch_shapes=[
            pltpu.SMEM(rank.shape, jnp.int32),
            pltpu.SMEM(lag.shape, jnp.int32),
            pltpu.VMEM((lags, steps, width), jnp.bfloat16),
            held,
            held,
            pltpu.SemaphoreType.DMA,
            pltpu.SemaphoreType.DMA,
            pltpu.SemaphoreType.DMA,
            pltpu.SemaphoreType.DMA((groups,)),
            pltpu.SemaphoreType.DMA((groups,)),
        ],
        compiler_params=pltpu.CompilerParams(vmem_limit_bytes=16 << 20),
        cost_estimate=pl.CostEstimate(
            flops=2 * rows * depth * width * (lags + 1) * steps,
            bytes_accessed=rows * depth * width * 4 + rows * steps * width * 2,
            transcendentals=0,
        ),
        name="far_half",
    )(core, rank, lag, history, right, left)


def plane_kernel(in_ref, out_ref):
    rows = 16
    for first in range(0, in_ref.shape[1], rows):
        part = slice(first, first + rows)
        total = in_ref[0, part].astype(jnp.float32)
        for source in range(1, in_ref.shape[0]):
            total = total + in_ref[source, part].astype(jnp.float32)
        for copy in range(out_ref.shape[0]):
            out_ref[copy, part] = total.astype(out_ref.dtype)


def plane_sum(arrived, copies):
    inside = pl.BlockSpec(memory_space=pltpu.VMEM)
    return pl.pallas_call(
        plane_kernel,
        out_shape=jax.ShapeDtypeStruct((copies, *arrived.shape[1:]), arrived.dtype),
        in_specs=[inside],
        out_specs=inside,
        compiler_params=pltpu.CompilerParams(vmem_limit_bytes=4 << 20),
        cost_estimate=pl.CostEstimate(
            flops=arrived.size, bytes_accessed=2 * arrived.size, transcendentals=0
        ),
        name="plane_sum",
    )(arrived)


def last_kernel(
    where_ref, own_ref, second_ref, first_ref, third_ref, incoming_ref, shifted_ref,
    out_ref, next_ref, whole_ref, front_ref, out_sem, next_sem
):
    row = where_ref[0]
    rows = own_ref.shape[0]
    for turn, piece in enumerate((own_ref, first_ref, second_ref, third_ref)):
        slot = lax.rem(row + 4 - turn, 4)
        at = pl.ds(pl.multiple_of(slot * rows, rows), rows)
        whole_ref[at] = piece[...]
        front_ref[at] = piece[...].astype(front_ref.dtype)
    whole = pltpu.make_async_copy(whole_ref, out_ref, out_sem)
    whole.start()
    front_ref[...] = jnp.where(where_ref[1] == 1, front_ref[...], incoming_ref[...])
    front = pltpu.make_async_copy(front_ref, next_ref.at[0], next_sem)
    front.start()
    whole.wait()
    front.wait()


def finish(where, pieces, incoming, shifted):
    steps, width = incoming.shape
    inside, outside = (pl.BlockSpec(memory_space=m) for m in (pltpu.VMEM, pltpu.HBM))
    return pl.pallas_call(
        last_kernel,
        out_shape=(
            jax.ShapeDtypeStruct((steps, width), jnp.float32),
            jax.ShapeDtypeStruct(shifted.shape, shifted.dtype),
        ),
        in_specs=[pl.BlockSpec(memory_space=pltpu.SMEM)] + [inside] * 5 + [outside],
        out_specs=(outside, outside),
        scratch_shapes=[
            pltpu.VMEM((steps, width), jnp.float32),
            pltpu.VMEM((steps, width), jnp.bfloat16),
            pltpu.SemaphoreType.DMA,
            pltpu.SemaphoreType.DMA,
        ],
        input_output_aliases={6: 1},
        compiler_params=pltpu.CompilerParams(vmem_limit_bytes=4 << 20),
        name="finish",
    )(where, *pieces, incoming, shifted)


def times(value, block_ref):
    return lax.dot_general(
        value, block_ref, (((1,), (1,)), ((), ())), preferred_element_type=jnp.float32
    )


def begin_kernel(c_ref, c_u_ref, inv_ref, own_ref, chip_ref, pack_ref, p_ref):
    value = c_ref[...].astype(jnp.bfloat16)
    beside = c_u_ref[...].astype(jnp.bfloat16)
    part = c_ref[...] - inv_ref[...] * (times(value, own_ref[...]) + times(beside, chip_ref[...]))
    pack_ref[0] = value
    pack_ref[1] = part.astype(jnp.bfloat16)
    p_ref[...] = part


def first_kernel(pack_ref, p_ref, got_ref, inv_ref, away_ref, back_ref, next_ref):
    mine = p_ref[...] - inv_ref[...] * times(got_ref[0], away_ref[...])
    other = got_ref[1].astype(jnp.float32) - times(pack_ref[0], back_ref[...])
    next_ref[0] = mine.astype(jnp.bfloat16)
    next_ref[1] = other.astype(jnp.bfloat16)


def second_kernel(
    next_ref, got_ref, c_ref, c_u_ref, inv_ref, inv_u_ref, own_ref, chip_ref, away_ref,
    own_u_ref, chip_u_ref, away_u_ref, pack_ref, p_ref
):
    mine, mine_away, other, other_away = next_ref[0], next_ref[1], got_ref[0], got_ref[1]
    total = times(mine, own_ref[...]) + times(other, chip_ref[...]) + times(mine_away, away_ref[...])
    total_u = (
        times(other, own_u_ref[...]) + times(mine, chip_u_ref[...]) + times(other_away, away_u_ref[...])
    )
    value = (c_ref[...] - inv_ref[...] * total).astype(jnp.bfloat16)
    beside = (c_u_ref[...] - inv_u_ref[...] * total_u).astype(jnp.bfloat16)
    part = c_ref[...] - inv_ref[...] * (times(value, own_ref[...]) + times(beside, chip_ref[...]))
    pack_ref[0] = value
    pack_ref[1] = part.astype(jnp.bfloat16)
    p_ref[...] = part


def end_kernel(p_ref, got_ref, inv_ref, away_ref, out_ref):
    out_ref[...] = p_ref[...] - inv_ref[...] * times(got_ref[0], away_ref[...])


def small_call(kernel, products, outs, *operands):
    inside = pl.BlockSpec(memory_space=pltpu.VMEM)
    rows, width = outs[0].shape[-2:]
    return pl.pallas_call(
        kernel,
        out_shape=outs,
        in_specs=[inside] * len(operands),
        out_specs=[inside] * len(outs),
        compiler_params=pltpu.CompilerParams(vmem_limit_bytes=8 << 20),
        cost_estimate=pl.CostEstimate(
            flops=2 * products * rows * width * width,
            bytes_accessed=2 * products * width * width,
            transcendentals=0,
        ),
    )(*operands)


def per_device(
    history, right_factor, left_factor, pair_rank, pair_lag, near_block, self_term, excitation
):
    _, time_steps, width = history.shape
    pairs, ranks, _ = right_factor.shape
    targets = 32
    depth = pairs // targets * ranks
    right = right_factor.reshape(targets // 2, 2, depth, width)
    left = left_factor.reshape(targets // 2, 2, depth, width)
    history_out, right, left, rank, lag = (
        pltpu.with_memory_space_constraint(v, pltpu.HBM)
        for v in (history, right, left, pair_rank[:, 0], pair_lag[:, 0])
    )
    core = lax.axis_index("c")
    swap = [(0, 1), (1, 0)]

    def half(which):
        return far_half(which.reshape(1), rank, lag, history_out, right, left, ranks)

    away = half(1 - core)
    came = lax.ppermute(away, "c", swap)
    mine = half(core)
    partial_value = (mine.astype(jnp.float32) + came.astype(jnp.float32)).astype(jnp.bfloat16)
    arrived = lax.all_to_all(partial_value.reshape(16, -1, width), ("x", "y"), 0, 0, tiled=True)
    incoming = lax.ppermute(history[-1], HIST, [(i, (i + 1) % 8) for i in range(8)])
    near_u = lax.ppermute(near_block, "c", swap)
    self_u = lax.ppermute(self_term[None, :], "c", swap)

    block = lax.axis_index(SPACE)
    inverse, inverse_u = 1.0 / self_term[None, :], 1.0 / self_u

    def sides(blocks, even, at):
        chip = jnp.where(even, blocks[2], blocks[0])
        away = jnp.where(even, blocks[0], blocks[2])
        away = jnp.where((at == 0) | (at == targets - 1), 0.0, away)
        return chip, away

    near_own = near_block[1]
    near_chip, near_away = sides(near_block, core == 0, block)
    toward = (inverse.reshape(width, 1) * near_away).astype(jnp.bfloat16)
    arrived, incoming, near_u, self_u, near_chip, near_away, toward = lax.optimization_barrier(
        (arrived, incoming, near_u, self_u, near_chip, near_away, toward)
    )
    inverse_u = 1.0 / self_u
    chip_u, away_u = sides(near_u, core == 1, block + 1 - 2 * core)
    shifted = jnp.concatenate([incoming[None], history[:-1]], axis=0)
    partner = {0: 0, targets - 1: targets - 1}
    for t in range(1, targets - 1, 2):
        partner[t], partner[t + 1] = t + 1, t
    between = []
    for t, other in partner.items():
        for y in range(4):
            between.append((t * 4 + y, other * 4 + (y ^ 1 if other == t else y)))

    def off_chip(value):
        return lax.ppermute(value, SPACE + ("y",), between)

    twice = plane_sum(arrived, 2).reshape(8, -1, width)
    arrived = lax.all_to_all(twice, ("zh", "zl"), 0, 0, tiled=True)
    back = off_chip(toward)
    back = jnp.where((block == 0) | (block == targets - 1), 0.0, back)
    arrived, incoming, shifted, chip_u, away_u = lax.optimization_barrier(
        (arrived, incoming, shifted, chip_u, away_u)
    )
    far_field = jnp.sum(arrived.astype(jnp.float32), axis=0)
    rows = time_steps // 4
    row = lax.axis_index("y")
    right_side = lax.dynamic_slice_in_dim(excitation, row * rows, rows, 0) - far_field

    c = right_side * inverse
    c_u = lax.ppermute(c, "c", swap)
    packed = jax.ShapeDtypeStruct((2, rows, width), jnp.bfloat16)
    single = jax.ShapeDtypeStruct((rows, width), jnp.float32)
    pack, part = small_call(begin_kernel, 2, (packed, single), c, c_u, inverse, near_own, near_chip)
    for _ in range((SWEEPS - 1) // 2):
        got = off_chip(pack)
        (both,) = small_call(first_kernel, 2, (packed,), pack, part, got, inverse, near_away, back)
        over = lax.ppermute(both, "c", swap)
        pack, part = small_call(
            second_kernel, 8, (packed, single),
            both, over, c, c_u, inverse, inverse_u, near_own, near_chip, near_away,
            near_u[1], chip_u, away_u,
        )
    got = off_chip(pack)
    (current,) = small_call(end_kernel, 1, (single,), part, got, inverse, near_away)

    pieces = [current]
    for step in (2, 1, 3):
        pieces.append(
            lax.ppermute(current, "y", [(i, (i + step) % 4) for i in range(4)])
        )
    oldest = ((lax.axis_index("zh") == 0) & (row == 0)).astype(jnp.int32)
    return finish(jnp.stack([row, oldest]), pieces, incoming, shifted)


def solution(mesh):
    fine = Mesh(mesh.devices.reshape(4, 4, 2, 2, 4), SPACE + HIST)
    in_specs = (
        P(HIST, None, SPACE),
        P(HIST, None, SPACE),
        P(HIST, None, SPACE),
        P(HIST, SPACE),
        P(HIST, SPACE),
        P(None, SPACE, None),
        P(SPACE),
        P(None, SPACE),
    )
    out_specs = (P(None, SPACE), P(HIST, None, SPACE))
    return jax.shard_map(
        per_device, mesh=fine, in_specs=in_specs, out_specs=out_specs, check_vma=False
    )
```

```python
import functools

import jax
import jax.numpy as jnp
from jax import lax
from jax.experimental import pallas as pl
from jax.experimental.pallas import tpu as pltpu
from jax.sharding import Mesh
from jax.sharding import PartitionSpec as P


SWEEPS = 8
SPACE = ("zl", "x", "c")
HIST = ("zh", "y")


def far_kernel(
    core_ref, rank_ref, lag_ref, hist_ref, right_ref, left_ref, out_ref,
    rank_buf, lag_buf, hist_buf, right_buf, left_buf,
    rank_sem, lag_sem, hist_sem, right_sem, left_sem, *, ranks
):
    groups, chips, depth, width = right_buf.shape
    lags, steps, _ = hist_buf.shape
    total = chips * depth
    core = core_ref[0]

    def brought(source, target, sem, group):
        return pltpu.make_async_copy(
            source.at[pl.ds(group * chips, chips), core], target.at[group], sem.at[group]
        )

    small = [
        pltpu.make_async_copy(rank_ref, rank_buf, rank_sem),
        pltpu.make_async_copy(lag_ref, lag_buf, lag_sem),
        pltpu.make_async_copy(hist_ref, hist_buf, hist_sem),
    ]
    for copy in small:
        copy.start()
    rights = [brought(right_ref, right_buf, right_sem, g) for g in range(groups)]
    lefts = [brought(left_ref, left_buf, left_sem, g) for g in range(groups)]
    for g in range(groups):
        rights[g].start()
        lefts[g].start()
    lane = lax.broadcasted_iota(jnp.int32, (1, total), 1)
    per = depth // ranks

    def chosen(group):
        column = jnp.full((1, total), -1, jnp.int32)
        for chip in range(chips):
            for k in range(per):
                pair = ((group * chips + chip) * 2 + core) * per + k
                first = (chip * per + k) * ranks
                inside = (lane >= first) & (lane < first + rank_buf[pair])
                column = jnp.where(inside, lag_buf[pair], column)
        every = lax.dot_general(
            hist_buf[...].reshape(lags * steps, width),
            right_buf[group].reshape(total, width),
            (((1,), (1,)), ((), ())),
            preferred_element_type=jnp.float32,
        )
        value = jnp.zeros((steps, total), jnp.float32)
        for lag in range(lags):
            value = jnp.where(column == lag, every[lag * steps : (lag + 1) * steps], value)
        return value.astype(jnp.bfloat16)

    def far(group, value):
        left = left_buf[group].reshape(total, width)
        for chip in range(chips):
            first, last = chip * depth, (chip + 1) * depth
            low, high = first // 128 * 128, -(-last // 128) * 128
            part = value[:, low:high]
            at = lax.broadcasted_iota(jnp.int32, part.shape, 1) + low
            part = jnp.where((at >= first) & (at < last), part, jnp.zeros_like(part))
            field = jnp.dot(part, left[low:high], preferred_element_type=jnp.float32)
            out_ref[chip, :, group] = field.reshape(out_ref.shape[1], -1, width).astype(out_ref.dtype)

    for copy in small:
        copy.wait()
    rights[0].wait()
    value = chosen(0)
    for g in range(groups):
        lefts[g].wait()
        ahead = None
        if g + 1 < groups:
            rights[g + 1].wait()
            ahead = chosen(g + 1)
        far(g, value)
        value = ahead


def far_half(core, rank, lag, history, right, left, ranks):
    rows, _, depth, width = right.shape
    lags, steps, _ = history.shape
    groups, chips, cuts = 4, 4, 4
    scalar = pl.BlockSpec(memory_space=pltpu.SMEM)
    outside = pl.BlockSpec(memory_space=pltpu.HBM)
    held = pltpu.VMEM((groups, chips, depth, width), jnp.bfloat16)
    return pl.pallas_call(
        functools.partial(far_kernel, ranks=ranks),
        out_shape=jax.ShapeDtypeStruct((chips, cuts, groups, steps // cuts, width), jnp.bfloat16),
        in_specs=[scalar] + [outside] * 5,
        out_specs=pl.BlockSpec(memory_space=pltpu.VMEM),
        scratch_shapes=[
            pltpu.SMEM(rank.shape, jnp.int32),
            pltpu.SMEM(lag.shape, jnp.int32),
            pltpu.VMEM((lags, steps, width), jnp.bfloat16),
            held,
            held,
            pltpu.SemaphoreType.DMA,
            pltpu.SemaphoreType.DMA,
            pltpu.SemaphoreType.DMA,
            pltpu.SemaphoreType.DMA((groups,)),
            pltpu.SemaphoreType.DMA((groups,)),
        ],
        compiler_params=pltpu.CompilerParams(vmem_limit_bytes=16 << 20),
        cost_estimate=pl.CostEstimate(
            flops=2 * rows * depth * width * (lags + 1) * steps,
            bytes_accessed=rows * depth * width * 4 + rows * steps * width * 2,
            transcendentals=0,
        ),
        name="far_half",
    )(core, rank, lag, history, right, left)


def plane_kernel(in_ref, out_ref):
    rows = 16
    for first in range(0, in_ref.shape[1], rows):
        part = slice(first, first + rows)
        total = in_ref[0, part].astype(jnp.float32)
        for source in range(1, in_ref.shape[0]):
            total = total + in_ref[source, part].astype(jnp.float32)
        for copy in range(out_ref.shape[0]):
            out_ref[copy, part] = total.astype(out_ref.dtype)


def plane_sum(arrived, copies):
    inside = pl.BlockSpec(memory_space=pltpu.VMEM)
    return pl.pallas_call(
        plane_kernel,
        out_shape=jax.ShapeDtypeStruct((copies, *arrived.shape[1:]), arrived.dtype),
        in_specs=[inside],
        out_specs=inside,
        compiler_params=pltpu.CompilerParams(vmem_limit_bytes=4 << 20),
        cost_estimate=pl.CostEstimate(
            flops=arrived.size, bytes_accessed=2 * arrived.size, transcendentals=0
        ),
        name="plane_sum",
    )(arrived)


def last_kernel(
    where_ref, own_ref, second_ref, first_ref, third_ref, incoming_ref, shifted_ref,
    out_ref, next_ref, whole_ref, front_ref, out_sem, next_sem
):
    row = where_ref[0]
    rows = own_ref.shape[0]
    for turn, piece in enumerate((own_ref, first_ref, second_ref, third_ref)):
        slot = lax.rem(row + 4 - turn, 4)
        at = pl.ds(pl.multiple_of(slot * rows, rows), rows)
        whole_ref[at] = piece[...]
        front_ref[at] = piece[...].astype(front_ref.dtype)
    whole = pltpu.make_async_copy(whole_ref, out_ref, out_sem)
    whole.start()
    front_ref[...] = jnp.where(where_ref[1] == 1, front_ref[...], incoming_ref[...])
    front = pltpu.make_async_copy(front_ref, next_ref.at[0], next_sem)
    front.start()
    whole.wait()
    front.wait()


def finish(where, pieces, incoming, shifted):
    steps, width = incoming.shape
    inside, outside = (pl.BlockSpec(memory_space=m) for m in (pltpu.VMEM, pltpu.HBM))
    return pl.pallas_call(
        last_kernel,
        out_shape=(
            jax.ShapeDtypeStruct((steps, width), jnp.float32),
            jax.ShapeDtypeStruct(shifted.shape, shifted.dtype),
        ),
        in_specs=[pl.BlockSpec(memory_space=pltpu.SMEM)] + [inside] * 5 + [outside],
        out_specs=(outside, outside),
        scratch_shapes=[
            pltpu.VMEM((steps, width), jnp.float32),
            pltpu.VMEM((steps, width), jnp.bfloat16),
            pltpu.SemaphoreType.DMA,
            pltpu.SemaphoreType.DMA,
        ],
        input_output_aliases={6: 1},
        compiler_params=pltpu.CompilerParams(vmem_limit_bytes=4 << 20),
        name="finish",
    )(where, *pieces, incoming, shifted)


def times(value, block_ref):
    return lax.dot_general(
        value, block_ref, (((1,), (1,)), ((), ())), preferred_element_type=jnp.float32
    )


def right_kernel(arrived_ref, given_ref, inv_ref, c_ref, value_ref):
    total = arrived_ref[0].astype(jnp.float32)
    for source in range(1, arrived_ref.shape[0]):
        total = total + arrived_ref[source].astype(jnp.float32)
    c = given_ref[...] - inv_ref[...] * total
    c_ref[...] = c
    value_ref[...] = c.astype(jnp.bfloat16)


def inner_kernel(value_ref, beside_ref, c_ref, inv_ref, own_ref, chip_ref, part_ref):
    beside = beside_ref[...].astype(jnp.bfloat16)
    total = times(value_ref[...], own_ref[...]) + times(beside, chip_ref[...])
    part_ref[...] = c_ref[...] - inv_ref[...] * total


def simple_kernel(part_ref, got_ref, inv_ref, away_ref, value_ref):
    value = part_ref[...] - inv_ref[...] * times(got_ref[...], away_ref[...])
    value_ref[...] = value.astype(jnp.bfloat16)


def one_kernel(value_ref, c_ref, inv_ref, own_ref, part_ref):
    part_ref[...] = c_ref[...] - inv_ref[...] * times(value_ref[...], own_ref[...])


def begin_kernel(value_ref, part_ref, beside_ref, inv_ref, chip_ref, pack_ref, p_ref):
    part = part_ref[...] - inv_ref[...] * times(beside_ref[...], chip_ref[...])
    pack_ref[0] = value_ref[...]
    pack_ref[1] = part.astype(jnp.bfloat16)
    p_ref[...] = part


def ahead_kernel(pack_ref, back_ref, out_ref):
    out_ref[...] = times(pack_ref[0], back_ref[...])


def first_kernel(known_ref, p_ref, got_ref, inv_ref, away_ref, next_ref):
    mine = p_ref[...] - inv_ref[...] * times(got_ref[0], away_ref[...])
    other = got_ref[1].astype(jnp.float32) - known_ref[...]
    next_ref[0] = mine.astype(jnp.bfloat16)
    next_ref[1] = other.astype(jnp.bfloat16)


def under_kernel(
    next_ref, c_ref, c_u_ref, inv_ref, inv_u_ref, own_ref, away_ref, chip_u_ref, part_ref, part_u_ref
):
    total = times(next_ref[0], own_ref[...]) + times(next_ref[1], away_ref[...])
    part_ref[...] = c_ref[...] - inv_ref[...] * total
    part_u_ref[...] = c_u_ref[...] - inv_u_ref[...] * times(next_ref[0], chip_u_ref[...])


def second_kernel(
    got_ref, part_ref, part_u_ref, c_ref, inv_ref, inv_u_ref, own_ref, chip_ref, own_u_ref,
    away_u_ref, pack_ref, p_ref
):
    value = part_ref[...] - inv_ref[...] * times(got_ref[0], chip_ref[...])
    total_u = times(got_ref[0], own_u_ref[...]) + times(got_ref[1], away_u_ref[...])
    value = value.astype(jnp.bfloat16)
    beside = (part_u_ref[...] - inv_u_ref[...] * total_u).astype(jnp.bfloat16)
    part = c_ref[...] - inv_ref[...] * (times(value, own_ref[...]) + times(beside, chip_ref[...]))
    pack_ref[0] = value
    pack_ref[1] = part.astype(jnp.bfloat16)
    p_ref[...] = part


def last_under_kernel(next_ref, c_ref, inv_ref, own_ref, away_ref, part_ref):
    total = times(next_ref[0], own_ref[...]) + times(next_ref[1], away_ref[...])
    part_ref[...] = c_ref[...] - inv_ref[...] * total


def end_kernel(part_ref, got_ref, inv_ref, chip_ref, out_ref):
    out_ref[...] = part_ref[...] - inv_ref[...] * times(got_ref[0], chip_ref[...])


def small_call(kernel, products, outs, *operands):
    inside = pl.BlockSpec(memory_space=pltpu.VMEM)
    rows, width = outs[0].shape[-2:]
    return pl.pallas_call(
        kernel,
        out_shape=outs,
        in_specs=[inside] * len(operands),
        out_specs=[inside] * len(outs),
        compiler_params=pltpu.CompilerParams(vmem_limit_bytes=8 << 20),
        cost_estimate=pl.CostEstimate(
            flops=2 * products * rows * width * width,
            bytes_accessed=2 * products * width * width,
            transcendentals=0,
        ),
    )(*operands)


def per_device(
    history, right_factor, left_factor, pair_rank, pair_lag, near_block, self_term, excitation
):
    _, time_steps, width = history.shape
    pairs, ranks, _ = right_factor.shape
    targets = 32
    depth = pairs // targets * ranks
    right = right_factor.reshape(targets // 2, 2, depth, width)
    left = left_factor.reshape(targets // 2, 2, depth, width)
    history_out, right, left, rank, lag = (
        pltpu.with_memory_space_constraint(v, pltpu.HBM)
        for v in (history, right, left, pair_rank[:, 0], pair_lag[:, 0])
    )
    core = lax.axis_index("c")
    swap = [(0, 1), (1, 0)]

    def half(which):
        return far_half(which.reshape(1), rank, lag, history_out, right, left, ranks)

    away = half(1 - core)
    came = lax.ppermute(away, "c", swap)
    mine = half(core)
    partial_value = (mine.astype(jnp.float32) + came.astype(jnp.float32)).astype(jnp.bfloat16)
    arrived = lax.all_to_all(partial_value.reshape(16, -1, width), ("x", "y"), 0, 0, tiled=True)
    incoming = lax.ppermute(history[-1], HIST, [(i, (i + 1) % 8) for i in range(8)])
    near_u = lax.ppermute(near_block, "c", swap)
    self_u = lax.ppermute(self_term[None, :], "c", swap)

    block = lax.axis_index(SPACE)
    inverse, inverse_u = 1.0 / self_term[None, :], 1.0 / self_u

    def sides(blocks, even, at):
        chip = jnp.where(even, blocks[2], blocks[0])
        away = jnp.where(even, blocks[0], blocks[2])
        away = jnp.where((at == 0) | (at == targets - 1), 0.0, away)
        return chip, away

    near_own = near_block[1]
    near_chip, near_away = sides(near_block, core == 0, block)
    toward = (inverse.reshape(width, 1) * near_away).astype(jnp.bfloat16)
    arrived, incoming, near_u, self_u, near_chip, near_away, toward = lax.optimization_barrier(
        (arrived, incoming, near_u, self_u, near_chip, near_away, toward)
    )
    inverse_u = 1.0 / self_u
    chip_u, away_u = sides(near_u, core == 1, block + 1 - 2 * core)
    shifted = jnp.concatenate([incoming[None], history[:-1]], axis=0)
    partner = {0: 0, targets - 1: targets - 1}
    for t in range(1, targets - 1, 2):
        partner[t], partner[t + 1] = t + 1, t
    between = []
    for t, other in partner.items():
        for y in range(4):
            between.append((t * 4 + y, other * 4 + (y ^ 1 if other == t else y)))

    def off_chip(value):
        return lax.ppermute(value, SPACE + ("y",), between)

    rows = time_steps // 4
    row = lax.axis_index("y")
    given = lax.dynamic_slice_in_dim(excitation, row * rows, rows, 0) * inverse
    twice = plane_sum(arrived, 2).reshape(8, -1, width)
    arrived = lax.all_to_all(twice, ("zh", "zl"), 0, 0, tiled=True)
    back = off_chip(toward)
    back = jnp.where((block == 0) | (block == targets - 1), 0.0, back)
    arrived, incoming, shifted, chip_u, away_u, given = lax.optimization_barrier(
        (arrived, incoming, shifted, chip_u, away_u, given)
    )
    packed = jax.ShapeDtypeStruct((2, rows, width), jnp.bfloat16)
    single = jax.ShapeDtypeStruct((rows, width), jnp.float32)
    rounded = jax.ShapeDtypeStruct((rows, width), jnp.bfloat16)
    c, value = small_call(right_kernel, 0, (single, rounded), arrived, given, inverse)
    got = off_chip(value)
    c_u = lax.ppermute(c, "c", swap)
    (part,) = small_call(inner_kernel, 2, (single,), value, c_u, c, inverse, near_own, near_chip)
    (value,) = small_call(simple_kernel, 1, (rounded,), part, got, inverse, near_away)
    beside = lax.ppermute(value, "c", swap)
    (part,) = small_call(one_kernel, 1, (single,), value, c, inverse, near_own)
    pack, part = small_call(
        begin_kernel, 1, (packed, single), value, part, beside, inverse, near_chip
    )
    for sweep in range(2, SWEEPS, 2):
        got = off_chip(pack)
        (known,) = small_call(ahead_kernel, 1, (single,), pack, back)
        (both,) = small_call(first_kernel, 1, (packed,), known, part, got, inverse, near_away)
        over = lax.ppermute(both, "c", swap)
        if sweep + 2 >= SWEEPS:
            (part,) = small_call(
                last_under_kernel, 2, (single,),
                both, c, inverse, near_own, near_away,
            )
            (current,) = small_call(end_kernel, 1, (single,), part, over, inverse, near_chip)
            break
        part, part_u = small_call(
            under_kernel, 3, (single, single),
            both, c, c_u, inverse, inverse_u, near_own, near_away, chip_u,
        )
        pack, part = small_call(
            second_kernel, 5, (packed, single),
            over, part, part_u, c, inverse, inverse_u, near_own, near_chip, near_u[1], away_u,
        )

    pieces = [current]
    for step in (2, 1, 3):
        pieces.append(
            lax.ppermute(current, "y", [(i, (i + step) % 4) for i in range(4)])
        )
    oldest = ((lax.axis_index("zh") == 0) & (row == 0)).astype(jnp.int32)
    return finish(jnp.stack([row, oldest]), pieces, incoming, shifted)


def solution(mesh):
    fine = Mesh(mesh.devices.reshape(4, 4, 2, 2, 4), SPACE + HIST)
    in_specs = (
        P(HIST, None, SPACE),
        P(HIST, None, SPACE),
        P(HIST, None, SPACE),
        P(HIST, SPACE),
        P(HIST, SPACE),
        P(None, SPACE, None),
        P(SPACE),
        P(None, SPACE),
    )
    out_specs = (P(None, SPACE), P(HIST, None, SPACE))
    return jax.shard_map(
        per_device, mesh=fine, in_specs=in_specs, out_specs=out_specs, check_vma=False
    )
```

```python
import functools

import jax
import jax.numpy as jnp
from jax import lax
from jax.experimental import pallas as pl
from jax.experimental.pallas import tpu as pltpu
from jax.sharding import Mesh
from jax.sharding import PartitionSpec as P


SWEEPS = 8
SPACE = ("zl", "x", "c")
HIST = ("zh", "y")


def far_kernel(
    core_ref, rank_ref, lag_ref, hist_ref, right_ref, left_ref, out_ref,
    rank_buf, lag_buf, hist_buf, right_buf, left_buf,
    rank_sem, lag_sem, hist_sem, right_sem, left_sem, *, ranks
):
    groups, chips, depth, width = right_buf.shape
    lags, steps, _ = hist_buf.shape
    total = chips * depth
    core = core_ref[0]

    def brought(source, target, sem, group):
        return pltpu.make_async_copy(
            source.at[pl.ds(group * chips, chips), core], target.at[group], sem.at[group]
        )

    small = [
        pltpu.make_async_copy(rank_ref, rank_buf, rank_sem),
        pltpu.make_async_copy(lag_ref, lag_buf, lag_sem),
        pltpu.make_async_copy(hist_ref, hist_buf, hist_sem),
    ]
    for copy in small:
        copy.start()
    rights = [brought(right_ref, right_buf, right_sem, g) for g in range(groups)]
    lefts = [brought(left_ref, left_buf, left_sem, g) for g in range(groups)]
    for g in range(groups):
        rights[g].start()
        lefts[g].start()
    lane = lax.broadcasted_iota(jnp.int32, (1, total), 1)
    per = depth // ranks

    def chosen(group):
        column = jnp.full((1, total), -1, jnp.int32)
        for chip in range(chips):
            for k in range(per):
                pair = ((group * chips + chip) * 2 + core) * per + k
                first = (chip * per + k) * ranks
                inside = (lane >= first) & (lane < first + rank_buf[pair])
                column = jnp.where(inside, lag_buf[pair], column)
        every = lax.dot_general(
            hist_buf[...].reshape(lags * steps, width),
            right_buf[group].reshape(total, width),
            (((1,), (1,)), ((), ())),
            preferred_element_type=jnp.float32,
        )
        value = jnp.zeros((steps, total), jnp.float32)
        for lag in range(lags):
            value = jnp.where(column == lag, every[lag * steps : (lag + 1) * steps], value)
        return value.astype(jnp.bfloat16)

    def far(group, value):
        left = left_buf[group].reshape(total, width)
        for chip in range(chips):
            first, last = chip * depth, (chip + 1) * depth
            low, high = first // 128 * 128, -(-last // 128) * 128
            part = value[:, low:high]
            at = lax.broadcasted_iota(jnp.int32, part.shape, 1) + low
            part = jnp.where((at >= first) & (at < last), part, jnp.zeros_like(part))
            field = jnp.dot(part, left[low:high], preferred_element_type=jnp.float32)
            at = group * (chips // 4) + chip // 4
            out_ref[chip % 4, :, at] = field.reshape(out_ref.shape[1], -1, width).astype(out_ref.dtype)

    for copy in small:
        copy.wait()
    rights[0].wait()
    value = chosen(0)
    for g in range(groups):
        lefts[g].wait()
        ahead = None
        if g + 1 < groups:
            rights[g + 1].wait()
            ahead = chosen(g + 1)
        far(g, value)
        value = ahead


def far_half(core, rank, lag, history, right, left, ranks):
    rows, _, depth, width = right.shape
    lags, steps, _ = history.shape
    groups, chips, cuts = 2, 16 // 2, 4
    scalar = pl.BlockSpec(memory_space=pltpu.SMEM)
    outside = pl.BlockSpec(memory_space=pltpu.HBM)
    held = pltpu.VMEM((groups, chips, depth, width), jnp.bfloat16)
    return pl.pallas_call(
        functools.partial(far_kernel, ranks=ranks),
        out_shape=jax.ShapeDtypeStruct((4, cuts, 4, steps // cuts, width), jnp.bfloat16),
        in_specs=[scalar] + [outside] * 5,
        out_specs=pl.BlockSpec(memory_space=pltpu.VMEM),
        scratch_shapes=[
            pltpu.SMEM(rank.shape, jnp.int32),
            pltpu.SMEM(lag.shape, jnp.int32),
            pltpu.VMEM((lags, steps, width), jnp.bfloat16),
            held,
            held,
            pltpu.SemaphoreType.DMA,
            pltpu.SemaphoreType.DMA,
            pltpu.SemaphoreType.DMA,
            pltpu.SemaphoreType.DMA((groups,)),
            pltpu.SemaphoreType.DMA((groups,)),
        ],
        compiler_params=pltpu.CompilerParams(vmem_limit_bytes=16 << 20),
        cost_estimate=pl.CostEstimate(
            flops=2 * rows * depth * width * (lags + 1) * steps,
            bytes_accessed=rows * depth * width * 4 + rows * steps * width * 2,
            transcendentals=0,
        ),
        name="far_half",
    )(core, rank, lag, history, right, left)


def halves_kernel(mine_ref, came_ref, out_ref, held_ref, sem):
    copies = []
    for piece in range(mine_ref.shape[0]):
        held_ref[piece] = mine_ref[piece] + came_ref[piece]
        copies.append(
            pltpu.make_async_copy(held_ref.at[piece], out_ref.at[piece], sem.at[piece])
        )
        copies[-1].start()
    for copy in copies:
        copy.wait()


def halves_sum(mine, came):
    inside = pl.BlockSpec(memory_space=pltpu.VMEM)
    return pl.pallas_call(
        halves_kernel,
        out_shape=jax.ShapeDtypeStruct(mine.shape, mine.dtype),
        in_specs=[inside, inside],
        out_specs=pl.BlockSpec(memory_space=pltpu.HBM),
        scratch_shapes=[
            pltpu.VMEM(mine.shape, mine.dtype),
            pltpu.SemaphoreType.DMA((mine.shape[0],)),
        ],
        compiler_params=pltpu.CompilerParams(vmem_limit_bytes=4 << 20),
        cost_estimate=pl.CostEstimate(
            flops=mine.size, bytes_accessed=6 * mine.size, transcendentals=0
        ),
        name="halves_sum",
    )(mine, came)


def plane_kernel(in_ref, out_ref):
    rows = 16
    for first in range(0, in_ref.shape[1], rows):
        part = slice(first, first + rows)
        total = in_ref[0, part].astype(jnp.float32)
        for source in range(1, in_ref.shape[0]):
            total = total + in_ref[source, part].astype(jnp.float32)
        for copy in range(out_ref.shape[0]):
            out_ref[copy, part] = total.astype(out_ref.dtype)


def plane_sum(arrived, copies):
    inside = pl.BlockSpec(memory_space=pltpu.VMEM)
    return pl.pallas_call(
        plane_kernel,
        out_shape=jax.ShapeDtypeStruct((copies, *arrived.shape[1:]), arrived.dtype),
        in_specs=[inside],
        out_specs=inside,
        compiler_params=pltpu.CompilerParams(vmem_limit_bytes=4 << 20),
        cost_estimate=pl.CostEstimate(
            flops=arrived.size, bytes_accessed=2 * arrived.size, transcendentals=0
        ),
        name="plane_sum",
    )(arrived)


def last_kernel(
    where_ref, own_ref, second_ref, first_ref, third_ref, incoming_ref, shifted_ref,
    out_ref, next_ref, front_ref, out_sem, next_sem
):
    row = where_ref[0]
    rows = own_ref.shape[0]
    copies = []
    for turn, piece in enumerate((own_ref, first_ref, second_ref, third_ref)):
        at = pl.ds(pl.multiple_of(lax.rem(row + 4 - turn, 4) * rows, rows), rows)
        copies.append(pltpu.make_async_copy(piece, out_ref.at[at], out_sem.at[turn]))
        copies[-1].start()
        front_ref[at] = piece[...].astype(front_ref.dtype)
    front_ref[...] = jnp.where(where_ref[1] == 1, front_ref[...], incoming_ref[...])
    copies.append(pltpu.make_async_copy(front_ref, next_ref.at[0], next_sem))
    copies[-1].start()
    for copy in copies:
        copy.wait()


def finish(where, pieces, incoming, shifted):
    steps, width = incoming.shape
    inside, outside = (pl.BlockSpec(memory_space=m) for m in (pltpu.VMEM, pltpu.HBM))
    return pl.pallas_call(
        last_kernel,
        out_shape=(
            jax.ShapeDtypeStruct((steps, width), jnp.float32),
            jax.ShapeDtypeStruct(shifted.shape, shifted.dtype),
        ),
        in_specs=[pl.BlockSpec(memory_space=pltpu.SMEM)] + [inside] * 5 + [outside],
        out_specs=(outside, outside),
        scratch_shapes=[
            pltpu.VMEM((steps, width), jnp.bfloat16),
            pltpu.SemaphoreType.DMA((4,)),
            pltpu.SemaphoreType.DMA,
        ],
        input_output_aliases={6: 1},
        compiler_params=pltpu.CompilerParams(vmem_limit_bytes=4 << 20),
        name="finish",
    )(where, *pieces, incoming, shifted)


def times(value, block_ref):
    return lax.dot_general(
        value, block_ref, (((1,), (1,)), ((), ())), preferred_element_type=jnp.float32
    )


def right_kernel(arrived_ref, given_ref, inv_ref, c_ref, value_ref):
    total = arrived_ref[0].astype(jnp.float32)
    for source in range(1, arrived_ref.shape[0]):
        total = total + arrived_ref[source].astype(jnp.float32)
    c = given_ref[...] - inv_ref[...] * total
    c_ref[...] = c
    value_ref[...] = c.astype(jnp.bfloat16)


def inner_kernel(value_ref, beside_ref, c_ref, inv_ref, own_ref, chip_ref, part_ref):
    beside = beside_ref[...].astype(jnp.bfloat16)
    total = times(value_ref[...], own_ref[...]) + times(beside, chip_ref[...])
    part_ref[...] = c_ref[...] - inv_ref[...] * total


def simple_kernel(part_ref, got_ref, inv_ref, away_ref, value_ref):
    value = part_ref[...] - inv_ref[...] * times(got_ref[...], away_ref[...])
    value_ref[...] = value.astype(jnp.bfloat16)


def one_kernel(value_ref, c_ref, inv_ref, own_ref, part_ref):
    part_ref[...] = c_ref[...] - inv_ref[...] * times(value_ref[...], own_ref[...])


def begin_kernel(value_ref, part_ref, beside_ref, inv_ref, chip_ref, pack_ref, p_ref):
    part = part_ref[...] - inv_ref[...] * times(beside_ref[...], chip_ref[...])
    pack_ref[0] = value_ref[...]
    pack_ref[1] = part.astype(jnp.bfloat16)
    p_ref[...] = part


def ahead_kernel(pack_ref, back_ref, out_ref):
    out_ref[...] = times(pack_ref[0], back_ref[...])


def first_kernel(known_ref, p_ref, got_ref, inv_ref, away_ref, next_ref):
    mine = p_ref[...] - inv_ref[...] * times(got_ref[0], away_ref[...])
    other = got_ref[1].astype(jnp.float32) - known_ref[...]
    next_ref[0] = mine.astype(jnp.bfloat16)
    next_ref[1] = other.astype(jnp.bfloat16)


def under_kernel(
    next_ref, c_ref, c_u_ref, inv_ref, inv_u_ref, own_ref, away_ref, chip_u_ref, part_ref, part_u_ref
):
    total = times(next_ref[0], own_ref[...]) + times(next_ref[1], away_ref[...])
    part_ref[...] = c_ref[...] - inv_ref[...] * total
    part_u_ref[...] = c_u_ref[...] - inv_u_ref[...] * times(next_ref[0], chip_u_ref[...])


def second_kernel(
    got_ref, part_ref, part_u_ref, c_ref, inv_ref, inv_u_ref, own_ref, chip_ref, own_u_ref,
    away_u_ref, pack_ref, p_ref
):
    value = part_ref[...] - inv_ref[...] * times(got_ref[0], chip_ref[...])
    total_u = times(got_ref[0], own_u_ref[...]) + times(got_ref[1], away_u_ref[...])
    value = value.astype(jnp.bfloat16)
    beside = (part_u_ref[...] - inv_u_ref[...] * total_u).astype(jnp.bfloat16)
    part = c_ref[...] - inv_ref[...] * (times(value, own_ref[...]) + times(beside, chip_ref[...]))
    pack_ref[0] = value
    pack_ref[1] = part.astype(jnp.bfloat16)
    p_ref[...] = part


def last_under_kernel(next_ref, c_ref, inv_ref, own_ref, away_ref, part_ref):
    total = times(next_ref[0], own_ref[...]) + times(next_ref[1], away_ref[...])
    part_ref[...] = c_ref[...] - inv_ref[...] * total


def end_kernel(part_ref, got_ref, inv_ref, chip_ref, out_ref):
    out_ref[...] = part_ref[...] - inv_ref[...] * times(got_ref[0], chip_ref[...])


def small_call(kernel, products, outs, *operands):
    inside = pl.BlockSpec(memory_space=pltpu.VMEM)
    rows, width = outs[0].shape[-2:]
    return pl.pallas_call(
        kernel,
        out_shape=outs,
        in_specs=[inside] * len(operands),
        out_specs=[inside] * len(outs),
        compiler_params=pltpu.CompilerParams(vmem_limit_bytes=8 << 20),
        cost_estimate=pl.CostEstimate(
            flops=2 * products * rows * width * width,
            bytes_accessed=2 * products * width * width,
            transcendentals=0,
        ),
    )(*operands)


def per_device(
    history, right_factor, left_factor, pair_rank, pair_lag, near_block, self_term, excitation
):
    _, time_steps, width = history.shape
    pairs, ranks, _ = right_factor.shape
    targets = 32
    depth = pairs // targets * ranks
    right = right_factor.reshape(targets // 2, 2, depth, width)
    left = left_factor.reshape(targets // 2, 2, depth, width)
    history_out, right, left, rank, lag = (
        pltpu.with_memory_space_constraint(v, pltpu.HBM)
        for v in (history, right, left, pair_rank[:, 0], pair_lag[:, 0])
    )
    core = lax.axis_index("c")
    swap = [(0, 1), (1, 0)]

    def half(which):
        return far_half(which.reshape(1), rank, lag, history_out, right, left, ranks)

    away = half(1 - core)
    came = lax.ppermute(away, "c", swap)
    mine = half(core)
    partial_value = halves_sum(mine, came)
    arrived = lax.all_to_all(partial_value.reshape(16, -1, width), ("x", "y"), 0, 0, tiled=True)
    incoming = lax.ppermute(history[-1], HIST, [(i, (i + 1) % 8) for i in range(8)])
    near_u = lax.ppermute(near_block, "c", swap)
    self_u = lax.ppermute(self_term[None, :], "c", swap)

    block = lax.axis_index(SPACE)
    inverse, inverse_u = 1.0 / self_term[None, :], 1.0 / self_u

    def sides(blocks, even, at):
        chip = jnp.where(even, blocks[2], blocks[0])
        away = jnp.where(even, blocks[0], blocks[2])
        away = jnp.where((at == 0) | (at == targets - 1), 0.0, away)
        return chip, away

    near_own = near_block[1]
    near_chip, near_away = sides(near_block, core == 0, block)
    toward = (inverse.reshape(width, 1) * near_away).astype(jnp.bfloat16)
    rows = time_steps // 4
    row = lax.axis_index("y")
    given = lax.dynamic_slice_in_dim(excitation, row * rows, rows, 0) * inverse
    (
        arrived, incoming, near_u, inverse_u, near_chip, near_away, toward, given
    ) = lax.optimization_barrier(
        (arrived, incoming, near_u, inverse_u, near_chip, near_away, toward, given)
    )
    chip_u, away_u = sides(near_u, core == 1, block + 1 - 2 * core)
    own_u = near_u[1]
    shifted = jnp.concatenate([incoming[None], history[:-1]], axis=0)
    partner = {0: 0, targets - 1: targets - 1}
    for t in range(1, targets - 1, 2):
        partner[t], partner[t + 1] = t + 1, t
    between = []
    for t, other in partner.items():
        for y in range(4):
            between.append((t * 4 + y, other * 4 + (y ^ 1 if other == t else y)))

    def off_chip(value):
        return lax.ppermute(value, SPACE + ("y",), between)

    twice = plane_sum(arrived, 2).reshape(8, -1, width)
    arrived = lax.all_to_all(twice, ("zh", "zl"), 0, 0, tiled=True)
    back = off_chip(toward)
    back = jnp.where((block == 0) | (block == targets - 1), 0.0, back)
    arrived, incoming, shifted, chip_u, away_u = lax.optimization_barrier(
        (arrived, incoming, shifted, chip_u, away_u)
    )
    packed = jax.ShapeDtypeStruct((2, rows, width), jnp.bfloat16)
    single = jax.ShapeDtypeStruct((rows, width), jnp.float32)
    rounded = jax.ShapeDtypeStruct((rows, width), jnp.bfloat16)
    c, value = small_call(right_kernel, 0, (single, rounded), arrived, given, inverse)
    got = off_chip(value)
    c_u = lax.ppermute(c, "c", swap)
    (part,) = small_call(inner_kernel, 2, (single,), value, c_u, c, inverse, near_own, near_chip)
    (value,) = small_call(simple_kernel, 1, (rounded,), part, got, inverse, near_away)
    beside = lax.ppermute(value, "c", swap)
    (part,) = small_call(one_kernel, 1, (single,), value, c, inverse, near_own)
    pack, part = small_call(
        begin_kernel, 1, (packed, single), value, part, beside, inverse, near_chip
    )
    for sweep in range(2, SWEEPS, 2):
        got = off_chip(pack)
        (known,) = small_call(ahead_kernel, 1, (single,), pack, back)
        (both,) = small_call(first_kernel, 1, (packed,), known, part, got, inverse, near_away)
        over = lax.ppermute(both, "c", swap)
        if sweep + 2 >= SWEEPS:
            (part,) = small_call(
                last_under_kernel, 2, (single,),
                both, c, inverse, near_own, near_away,
            )
            (current,) = small_call(end_kernel, 1, (single,), part, over, inverse, near_chip)
            break
        part, part_u = small_call(
            under_kernel, 3, (single, single),
            both, c, c_u, inverse, inverse_u, near_own, near_away, chip_u,
        )
        pack, part = small_call(
            second_kernel, 5, (packed, single),
            over, part, part_u, c, inverse, inverse_u, near_own, near_chip, own_u, away_u,
        )

    pieces = [current]
    for step in (2, 1, 3):
        pieces.append(
            lax.ppermute(current, "y", [(i, (i + step) % 4) for i in range(4)])
        )
    oldest = ((lax.axis_index("zh") == 0) & (row == 0)).astype(jnp.int32)
    return finish(jnp.stack([row, oldest]), pieces, incoming, shifted)


def solution(mesh):
    fine = Mesh(mesh.devices.reshape(4, 4, 2, 2, 4), SPACE + HIST)
    in_specs = (
        P(HIST, None, SPACE),
        P(HIST, None, SPACE),
        P(HIST, None, SPACE),
        P(HIST, SPACE),
        P(HIST, SPACE),
        P(None, SPACE, None),
        P(SPACE),
        P(None, SPACE),
    )
    out_specs = (P(None, SPACE), P(HIST, None, SPACE))
    return jax.shard_map(
        per_device, mesh=fine, in_specs=in_specs, out_specs=out_specs, check_vma=False
    )
```

```python
import functools

import jax
import jax.numpy as jnp
from jax import lax
from jax.experimental import pallas as pl
from jax.experimental.pallas import tpu as pltpu
from jax.sharding import Mesh
from jax.sharding import PartitionSpec as P


SWEEPS = 8
SPACE = ("zl", "x", "c")
HIST = ("zh", "y")


def far_kernel(
    core_ref, rank_ref, lag_ref, hist_ref, right_ref, left_ref, out_ref,
    rank_buf, lag_buf, hist_buf, right_buf, left_buf,
    rank_sem, lag_sem, hist_sem, right_sem, left_sem, *, ranks
):
    groups, chips, depth, width = right_buf.shape
    lags, steps, _ = hist_buf.shape
    total = chips * depth
    core = core_ref[0]

    def brought(source, target, sem, group):
        return pltpu.make_async_copy(
            source.at[pl.ds(group * chips, chips), core], target.at[group], sem.at[group]
        )

    small = [
        pltpu.make_async_copy(rank_ref, rank_buf, rank_sem),
        pltpu.make_async_copy(lag_ref, lag_buf, lag_sem),
        pltpu.make_async_copy(hist_ref, hist_buf, hist_sem),
    ]
    for copy in small:
        copy.start()
    rights = [brought(right_ref, right_buf, right_sem, g) for g in range(groups)]
    lefts = [brought(left_ref, left_buf, left_sem, g) for g in range(groups)]
    for g in range(groups):
        rights[g].start()
        lefts[g].start()
    lane = lax.broadcasted_iota(jnp.int32, (1, total), 1)
    per = depth // ranks

    def chosen(group):
        column = jnp.full((1, total), -1, jnp.int32)
        for chip in range(chips):
            for k in range(per):
                pair = ((group * chips + chip) * 2 + core) * per + k
                first = (chip * per + k) * ranks
                inside = (lane >= first) & (lane < first + rank_buf[pair])
                column = jnp.where(inside, lag_buf[pair], column)
        every = lax.dot_general(
            hist_buf[...].reshape(lags * steps, width),
            right_buf[group].reshape(total, width),
            (((1,), (1,)), ((), ())),
            preferred_element_type=jnp.float32,
        )
        value = jnp.zeros((steps, total), jnp.float32)
        for lag in range(lags):
            value = jnp.where(column == lag, every[lag * steps : (lag + 1) * steps], value)
        return value.astype(jnp.bfloat16)

    def far(group, value):
        left = left_buf[group].reshape(total, width)
        for chip in range(chips):
            first, last = chip * depth, (chip + 1) * depth
            low, high = first // 128 * 128, -(-last // 128) * 128
            part = value[:, low:high]
            at = lax.broadcasted_iota(jnp.int32, part.shape, 1) + low
            part = jnp.where((at >= first) & (at < last), part, jnp.zeros_like(part))
            field = jnp.dot(part, left[low:high], preferred_element_type=jnp.float32)
            at = group * (chips // 4) + chip // 4
            out_ref[chip % 4, :, at] = field.reshape(out_ref.shape[1], -1, width).astype(out_ref.dtype)

    for copy in small:
        copy.wait()
    rights[0].wait()
    value = chosen(0)
    for g in range(groups):
        lefts[g].wait()
        ahead = None
        if g + 1 < groups:
            rights[g + 1].wait()
            ahead = chosen(g + 1)
        far(g, value)
        value = ahead


def far_half(core, rank, lag, history, right, left, ranks):
    rows, _, depth, width = right.shape
    lags, steps, _ = history.shape
    groups, chips, cuts = 2, 16 // 2, 4
    scalar = pl.BlockSpec(memory_space=pltpu.SMEM)
    outside = pl.BlockSpec(memory_space=pltpu.HBM)
    held = pltpu.VMEM((groups, chips, depth, width), jnp.bfloat16)
    return pl.pallas_call(
        functools.partial(far_kernel, ranks=ranks),
        out_shape=jax.ShapeDtypeStruct((4, cuts, 4, steps // cuts, width), jnp.bfloat16),
        in_specs=[scalar] + [outside] * 5,
        out_specs=pl.BlockSpec(memory_space=pltpu.VMEM),
        scratch_shapes=[
            pltpu.SMEM(rank.shape, jnp.int32),
            pltpu.SMEM(lag.shape, jnp.int32),
            pltpu.VMEM((lags, steps, width), jnp.bfloat16),
            held,
            held,
            pltpu.SemaphoreType.DMA,
            pltpu.SemaphoreType.DMA,
            pltpu.SemaphoreType.DMA,
            pltpu.SemaphoreType.DMA((groups,)),
            pltpu.SemaphoreType.DMA((groups,)),
        ],
        compiler_params=pltpu.CompilerParams(vmem_limit_bytes=16 << 20),
        cost_estimate=pl.CostEstimate(
            flops=2 * rows * depth * width * (lags + 1) * steps,
            bytes_accessed=rows * depth * width * 4 + rows * steps * width * 2,
            transcendentals=0,
        ),
        name="far_half",
    )(core, rank, lag, history, right, left)


def halves_kernel(mine_ref, came_ref, out_ref, held_ref, sem):
    copies = []
    for piece in range(mine_ref.shape[0]):
        held_ref[piece] = mine_ref[piece] + came_ref[piece]
        copies.append(
            pltpu.make_async_copy(held_ref.at[piece], out_ref.at[piece], sem.at[piece])
        )
        copies[-1].start()
    for copy in copies:
        copy.wait()


def halves_sum(mine, came):
    inside = pl.BlockSpec(memory_space=pltpu.VMEM)
    return pl.pallas_call(
        halves_kernel,
        out_shape=jax.ShapeDtypeStruct(mine.shape, mine.dtype),
        in_specs=[inside, inside],
        out_specs=pl.BlockSpec(memory_space=pltpu.HBM),
        scratch_shapes=[
            pltpu.VMEM(mine.shape, mine.dtype),
            pltpu.SemaphoreType.DMA((mine.shape[0],)),
        ],
        compiler_params=pltpu.CompilerParams(vmem_limit_bytes=4 << 20),
        cost_estimate=pl.CostEstimate(
            flops=mine.size, bytes_accessed=6 * mine.size, transcendentals=0
        ),
        name="halves_sum",
    )(mine, came)


def plane_kernel(in_ref, out_ref, held_ref, sem):
    copies = []
    pieces, rows, _ = held_ref.shape
    for piece in range(pieces):
        part = slice(piece * rows, (piece + 1) * rows)
        total = in_ref[0, part].astype(jnp.float32)
        for source in range(1, in_ref.shape[0]):
            total = total + in_ref[source, part].astype(jnp.float32)
        held_ref[piece] = total.astype(held_ref.dtype)
        for twin in range(out_ref.shape[0]):
            copies.append(
                pltpu.make_async_copy(
                    held_ref.at[piece], out_ref.at[twin, part], sem.at[twin, piece]
                )
            )
            copies[-1].start()
    for copy in copies:
        copy.wait()


def plane_sum(arrived, copies):
    pieces = 4
    return pl.pallas_call(
        plane_kernel,
        out_shape=jax.ShapeDtypeStruct((copies, *arrived.shape[1:]), arrived.dtype),
        in_specs=[pl.BlockSpec(memory_space=pltpu.VMEM)],
        out_specs=pl.BlockSpec(memory_space=pltpu.HBM),
        scratch_shapes=[
            pltpu.VMEM((pieces, arrived.shape[1] // pieces, arrived.shape[2]), arrived.dtype),
            pltpu.SemaphoreType.DMA((copies, pieces)),
        ],
        compiler_params=pltpu.CompilerParams(vmem_limit_bytes=4 << 20),
        cost_estimate=pl.CostEstimate(
            flops=arrived.size, bytes_accessed=2 * arrived.size, transcendentals=0
        ),
        name="plane_sum",
    )(arrived)


def last_kernel(
    where_ref, own_ref, second_ref, first_ref, third_ref, incoming_ref, shifted_ref,
    out_ref, next_ref, front_ref, out_sem, next_sem
):
    row = where_ref[0]
    rows = own_ref.shape[0]
    copies = []
    for turn, piece in enumerate((own_ref, first_ref, second_ref, third_ref)):
        at = pl.ds(pl.multiple_of(lax.rem(row + 4 - turn, 4) * rows, rows), rows)
        copies.append(pltpu.make_async_copy(piece, out_ref.at[at], out_sem.at[turn]))
        copies[-1].start()
        front_ref[at] = piece[...].astype(front_ref.dtype)
    front_ref[...] = jnp.where(where_ref[1] == 1, front_ref[...], incoming_ref[...])
    copies.append(pltpu.make_async_copy(front_ref, next_ref.at[0], next_sem))
    copies[-1].start()
    for copy in copies:
        copy.wait()


def finish(where, pieces, incoming, shifted):
    steps, width = incoming.shape
    inside, outside = (pl.BlockSpec(memory_space=m) for m in (pltpu.VMEM, pltpu.HBM))
    return pl.pallas_call(
        last_kernel,
        out_shape=(
            jax.ShapeDtypeStruct((steps, width), jnp.float32),
            jax.ShapeDtypeStruct(shifted.shape, shifted.dtype),
        ),
        in_specs=[pl.BlockSpec(memory_space=pltpu.SMEM)] + [inside] * 5 + [outside],
        out_specs=(outside, outside),
        scratch_shapes=[
            pltpu.VMEM((steps, width), jnp.bfloat16),
            pltpu.SemaphoreType.DMA((4,)),
            pltpu.SemaphoreType.DMA,
        ],
        input_output_aliases={6: 1},
        compiler_params=pltpu.CompilerParams(vmem_limit_bytes=4 << 20),
        name="finish",
    )(where, *pieces, incoming, shifted)


def times(value, block_ref):
    return lax.dot_general(
        value, block_ref, (((1,), (1,)), ((), ())), preferred_element_type=jnp.float32
    )


def right_kernel(arrived_ref, given_ref, inv_ref, c_ref, value_ref):
    total = arrived_ref[0].astype(jnp.float32)
    for source in range(1, arrived_ref.shape[0]):
        total = total + arrived_ref[source].astype(jnp.float32)
    c = given_ref[...] - inv_ref[...] * total
    c_ref[...] = c
    value_ref[...] = c.astype(jnp.bfloat16)


def inner_kernel(value_ref, beside_ref, c_ref, inv_ref, own_ref, chip_ref, part_ref):
    beside = beside_ref[...].astype(jnp.bfloat16)
    total = times(value_ref[...], own_ref[...]) + times(beside, chip_ref[...])
    part_ref[...] = c_ref[...] - inv_ref[...] * total


def simple_kernel(part_ref, got_ref, inv_ref, away_ref, value_ref):
    value = part_ref[...] - inv_ref[...] * times(got_ref[...], away_ref[...])
    value_ref[...] = value.astype(jnp.bfloat16)


def one_kernel(value_ref, c_ref, inv_ref, own_ref, part_ref):
    part_ref[...] = c_ref[...] - inv_ref[...] * times(value_ref[...], own_ref[...])


def begin_kernel(value_ref, part_ref, beside_ref, inv_ref, chip_ref, pack_ref, p_ref):
    part = part_ref[...] - inv_ref[...] * times(beside_ref[...], chip_ref[...])
    pack_ref[0] = value_ref[...]
    pack_ref[1] = part.astype(jnp.bfloat16)
    p_ref[...] = part


def ahead_kernel(pack_ref, back_ref, out_ref):
    out_ref[...] = times(pack_ref[0], back_ref[...])


def first_kernel(known_ref, p_ref, got_ref, inv_ref, away_ref, next_ref):
    mine = p_ref[...] - inv_ref[...] * times(got_ref[0], away_ref[...])
    other = got_ref[1].astype(jnp.float32) - known_ref[...]
    next_ref[0] = mine.astype(jnp.bfloat16)
    next_ref[1] = other.astype(jnp.bfloat16)


def under_kernel(
    next_ref, c_ref, c_u_ref, inv_ref, inv_u_ref, own_ref, away_ref, chip_u_ref, part_ref, part_u_ref
):
    total = times(next_ref[0], own_ref[...]) + times(next_ref[1], away_ref[...])
    part_ref[...] = c_ref[...] - inv_ref[...] * total
    part_u_ref[...] = c_u_ref[...] - inv_u_ref[...] * times(next_ref[0], chip_u_ref[...])


def second_kernel(
    got_ref, part_ref, part_u_ref, c_ref, inv_ref, inv_u_ref, own_ref, chip_ref, own_u_ref,
    away_u_ref, pack_ref, p_ref
):
    value = part_ref[...] - inv_ref[...] * times(got_ref[0], chip_ref[...])
    total_u = times(got_ref[0], own_u_ref[...]) + times(got_ref[1], away_u_ref[...])
    value = value.astype(jnp.bfloat16)
    beside = (part_u_ref[...] - inv_u_ref[...] * total_u).astype(jnp.bfloat16)
    part = c_ref[...] - inv_ref[...] * (times(value, own_ref[...]) + times(beside, chip_ref[...]))
    pack_ref[0] = value
    pack_ref[1] = part.astype(jnp.bfloat16)
    p_ref[...] = part


def last_under_kernel(next_ref, c_ref, inv_ref, own_ref, away_ref, part_ref):
    total = times(next_ref[0], own_ref[...]) + times(next_ref[1], away_ref[...])
    part_ref[...] = c_ref[...] - inv_ref[...] * total


def end_kernel(part_ref, got_ref, inv_ref, chip_ref, out_ref):
    out_ref[...] = part_ref[...] - inv_ref[...] * times(got_ref[0], chip_ref[...])


def small_call(kernel, products, outs, *operands):
    inside = pl.BlockSpec(memory_space=pltpu.VMEM)
    rows, width = outs[0].shape[-2:]
    return pl.pallas_call(
        kernel,
        out_shape=outs,
        in_specs=[inside] * len(operands),
        out_specs=[inside] * len(outs),
        compiler_params=pltpu.CompilerParams(vmem_limit_bytes=8 << 20),
        cost_estimate=pl.CostEstimate(
            flops=2 * products * rows * width * width,
            bytes_accessed=2 * products * width * width,
            transcendentals=0,
        ),
    )(*operands)


def per_device(
    history, right_factor, left_factor, pair_rank, pair_lag, near_block, self_term, excitation
):
    _, time_steps, width = history.shape
    pairs, ranks, _ = right_factor.shape
    targets = 32
    depth = pairs // targets * ranks
    right = right_factor.reshape(targets // 2, 2, depth, width)
    left = left_factor.reshape(targets // 2, 2, depth, width)
    history_out, right, left, rank, lag = (
        pltpu.with_memory_space_constraint(v, pltpu.HBM)
        for v in (history, right, left, pair_rank[:, 0], pair_lag[:, 0])
    )
    core = lax.axis_index("c")
    swap = [(0, 1), (1, 0)]

    def half(which):
        return far_half(which.reshape(1), rank, lag, history_out, right, left, ranks)

    away = half(1 - core)
    came = lax.ppermute(away, "c", swap)
    mine = half(core)
    partial_value = halves_sum(mine, came)
    arrived = lax.all_to_all(partial_value.reshape(16, -1, width), ("x", "y"), 0, 0, tiled=True)
    incoming = lax.ppermute(history[-1], HIST, [(i, (i + 1) % 8) for i in range(8)])
    near_u = lax.ppermute(near_block, "c", swap)
    self_u = lax.ppermute(self_term[None, :], "c", swap)

    block = lax.axis_index(SPACE)
    inverse, inverse_u = 1.0 / self_term[None, :], 1.0 / self_u

    def sides(blocks, even, at):
        chip = jnp.where(even, blocks[2], blocks[0])
        away = jnp.where(even, blocks[0], blocks[2])
        away = jnp.where((at == 0) | (at == targets - 1), 0.0, away)
        return chip, away

    near_own = near_block[1]
    near_chip, near_away = sides(near_block, core == 0, block)
    toward = (inverse.reshape(width, 1) * near_away).astype(jnp.bfloat16)
    rows = time_steps // 4
    row = lax.axis_index("y")
    given = lax.dynamic_slice_in_dim(excitation, row * rows, rows, 0) * inverse
    (
        arrived, incoming, near_u, inverse_u, near_chip, near_away, toward, given
    ) = lax.optimization_barrier(
        (arrived, incoming, near_u, inverse_u, near_chip, near_away, toward, given)
    )
    chip_u, away_u = sides(near_u, core == 1, block + 1 - 2 * core)
    own_u = near_u[1]
    shifted = jnp.concatenate([incoming[None], history[:-1]], axis=0)
    partner = {0: 0, targets - 1: targets - 1}
    for t in range(1, targets - 1, 2):
        partner[t], partner[t + 1] = t + 1, t
    between = []
    for t, other in partner.items():
        for y in range(4):
            between.append((t * 4 + y, other * 4 + (y ^ 1 if other == t else y)))

    def off_chip(value):
        return lax.ppermute(value, SPACE + ("y",), between)

    twice = plane_sum(arrived, 2).reshape(8, -1, width)
    arrived = lax.all_to_all(twice, ("zh", "zl"), 0, 0, tiled=True)
    back = off_chip(toward)
    back = jnp.where((block == 0) | (block == targets - 1), 0.0, back)
    arrived, incoming, shifted, chip_u, away_u = lax.optimization_barrier(
        (arrived, incoming, shifted, chip_u, away_u)
    )
    packed = jax.ShapeDtypeStruct((2, rows, width), jnp.bfloat16)
    single = jax.ShapeDtypeStruct((rows, width), jnp.float32)
    rounded = jax.ShapeDtypeStruct((rows, width), jnp.bfloat16)
    c, value = small_call(right_kernel, 0, (single, rounded), arrived, given, inverse)
    got = off_chip(value)
    c_u = lax.ppermute(c, "c", swap)
    (part,) = small_call(inner_kernel, 2, (single,), value, c_u, c, inverse, near_own, near_chip)
    (value,) = small_call(simple_kernel, 1, (rounded,), part, got, inverse, near_away)
    beside = lax.ppermute(value, "c", swap)
    (part,) = small_call(one_kernel, 1, (single,), value, c, inverse, near_own)
    pack, part = small_call(
        begin_kernel, 1, (packed, single), value, part, beside, inverse, near_chip
    )
    for sweep in range(2, SWEEPS, 2):
        got = off_chip(pack)
        (known,) = small_call(ahead_kernel, 1, (single,), pack, back)
        (both,) = small_call(first_kernel, 1, (packed,), known, part, got, inverse, near_away)
        over = lax.ppermute(both, "c", swap)
        if sweep + 2 >= SWEEPS:
            (part,) = small_call(
                last_under_kernel, 2, (single,),
                both, c, inverse, near_own, near_away,
            )
            (current,) = small_call(end_kernel, 1, (single,), part, over, inverse, near_chip)
            break
        part, part_u = small_call(
            under_kernel, 3, (single, single),
            both, c, c_u, inverse, inverse_u, near_own, near_away, chip_u,
        )
        pack, part = small_call(
            second_kernel, 5, (packed, single),
            over, part, part_u, c, inverse, inverse_u, near_own, near_chip, own_u, away_u,
        )

    pieces = [current]
    for step in (2, 1, 3):
        pieces.append(
            lax.ppermute(current, "y", [(i, (i + step) % 4) for i in range(4)])
        )
    oldest = ((lax.axis_index("zh") == 0) & (row == 0)).astype(jnp.int32)
    return finish(jnp.stack([row, oldest]), pieces, incoming, shifted)


def solution(mesh):
    fine = Mesh(mesh.devices.reshape(4, 4, 2, 2, 4), SPACE + HIST)
    in_specs = (
        P(HIST, None, SPACE),
        P(HIST, None, SPACE),
        P(HIST, None, SPACE),
        P(HIST, SPACE),
        P(HIST, SPACE),
        P(None, SPACE, None),
        P(SPACE),
        P(None, SPACE),
    )
    out_specs = (P(None, SPACE), P(HIST, None, SPACE))
    return jax.shard_map(
        per_device, mesh=fine, in_specs=in_specs, out_specs=out_specs, check_vma=False
    )
```

```python
import functools

import jax
import jax.numpy as jnp
from jax import lax
from jax.experimental import pallas as pl
from jax.experimental.pallas import tpu as pltpu
from jax.sharding import Mesh
from jax.sharding import PartitionSpec as P


SWEEPS = 8
SPACE = ("zl", "x", "c")
HIST = ("zh", "y")


GROUPS = 2


def brought(source, target, sem, group, core):
    chips = target.shape[0]
    return pltpu.make_async_copy(source.at[pl.ds(group * chips, chips), core], target, sem)


def column_of(group, core, rank_ref, lag_ref, chips, depth, ranks):
    lane = lax.broadcasted_iota(jnp.int32, (1, chips * depth), 1)
    column = jnp.full((1, chips * depth), -1, jnp.int32)
    per = depth // ranks
    for chip in range(chips):
        for k in range(per):
            pair = ((group * chips + chip) * 2 + core) * per + k
            first = (chip * per + k) * ranks
            inside = (lane >= first) & (lane < first + rank_ref[pair])
            column = jnp.where(inside, lag_ref[pair], column)
    return column


def chosen(hist_ref, right_ref, column):
    lags, steps, width = hist_ref.shape
    every = lax.dot_general(
        hist_ref[...].reshape(lags * steps, width),
        right_ref[...].reshape(-1, width),
        (((1,), (1,)), ((), ())),
        preferred_element_type=jnp.float32,
    )
    value = jnp.zeros((steps, every.shape[1]), jnp.float32)
    for lag in range(lags):
        value = jnp.where(column == lag, every[lag * steps : (lag + 1) * steps], value)
    return value.astype(jnp.bfloat16)


def far(group, value, left_ref, out_ref):
    chips, depth, width = left_ref.shape
    left = left_ref[...].reshape(chips * depth, width)
    for chip in range(chips):
        first, last = chip * depth, (chip + 1) * depth
        low, high = first // 128 * 128, -(-last // 128) * 128
        part = value[:, low:high]
        at = lax.broadcasted_iota(jnp.int32, part.shape, 1) + low
        part = jnp.where((at >= first) & (at < last), part, jnp.zeros_like(part))
        field = jnp.dot(part, left[low:high], preferred_element_type=jnp.float32)
        line = group * (chips // 4) + chip // 4
        out_ref[chip % 4, :, line] = field.reshape(out_ref.shape[1], -1, width).astype(out_ref.dtype)


def away_kernel(
    core_ref, rank_ref, lag_ref, hist_ref, right_ref, left_ref,
    out_ref, hist_buf, right_own, left_own, columns_ref,
    rank_buf, lag_buf, right_buf, left_buf, small_sem, right_sem, left_sem, *, ranks
):
    groups, chips, depth, _ = right_buf.shape
    core = core_ref[0]
    other = 1 - core
    small = [
        pltpu.make_async_copy(rank_ref, rank_buf, small_sem.at[0]),
        pltpu.make_async_copy(lag_ref, lag_buf, small_sem.at[1]),
        pltpu.make_async_copy(hist_ref, hist_buf, small_sem.at[2]),
    ]
    for copy in small:
        copy.start()
    rights = [
        brought(right_ref, right_buf.at[g], right_sem.at[g], g, other) for g in range(groups)
    ]
    lefts = [brought(left_ref, left_buf.at[g], left_sem.at[g], g, other) for g in range(groups)]
    for g in range(groups):
        rights[g].start()
        lefts[g].start()
    late = [
        brought(right_ref, right_own, right_sem.at[groups], 0, core),
        brought(left_ref, left_own, left_sem.at[groups], 0, core),
    ]
    for copy in late:
        copy.start()
    small[0].wait()
    small[1].wait()
    columns = []
    for g in range(groups):
        columns.append(column_of(g, other, rank_buf, lag_buf, chips, depth, ranks))
        columns_ref[g : g + 1] = column_of(g, core, rank_buf, lag_buf, chips, depth, ranks)
    small[2].wait()
    rights[0].wait()
    value = chosen(hist_buf, right_buf.at[0], columns[0])
    for g in range(groups):
        lefts[g].wait()
        ahead = None
        if g + 1 < groups:
            rights[g + 1].wait()
            ahead = chosen(hist_buf, right_buf.at[g + 1], columns[g + 1])
        far(g, value, left_buf.at[g], out_ref)
        value = ahead
    for copy in late:
        copy.wait()


def own_kernel(
    core_ref, hist_ref, right_own, left_own, columns_ref, right_ref, left_ref, out_ref,
    right_buf, left_buf, right_sem, left_sem
):
    core = core_ref[0]
    groups = right_buf.shape[0] + 1
    rights = [
        brought(right_ref, right_buf.at[g], right_sem.at[g], g + 1, core) for g in range(groups - 1)
    ]
    lefts = [
        brought(left_ref, left_buf.at[g], left_sem.at[g], g + 1, core) for g in range(groups - 1)
    ]
    for g in range(groups - 1):
        rights[g].start()
        lefts[g].start()
    value = chosen(hist_ref, right_own, columns_ref[0:1])
    for g in range(groups):
        if g > 0:
            lefts[g - 1].wait()
        ahead = None
        if g + 1 < groups:
            rights[g].wait()
            ahead = chosen(hist_ref, right_buf.at[g], columns_ref[g + 1 : g + 2])
        far(g, value, left_own if g == 0 else left_buf.at[g - 1], out_ref)
        value = ahead


def far_halves(core, rank, lag, history, right, left, ranks):
    rows, _, depth, width = right.shape
    lags, steps, _ = history.shape
    chips = rows // GROUPS
    field = jax.ShapeDtypeStruct((4, 4, 4, steps // 4, width), jnp.bfloat16)
    block = (chips, depth, width)
    scalar = pl.BlockSpec(memory_space=pltpu.SMEM)
    inside = pl.BlockSpec(memory_space=pltpu.VMEM)
    outside = pl.BlockSpec(memory_space=pltpu.HBM)
    cost = pl.CostEstimate(
        flops=2 * rows * depth * width * (lags + 1) * steps,
        bytes_accessed=rows * depth * width * 4 + rows * steps * width * 2,
        transcendentals=0,
    )
    semaphores = pltpu.SemaphoreType.DMA
    away, hist_buf, right_own, left_own, columns = pl.pallas_call(
        functools.partial(away_kernel, ranks=ranks),
        out_shape=(
            field,
            jax.ShapeDtypeStruct(history.shape, history.dtype),
            jax.ShapeDtypeStruct(block, right.dtype),
            jax.ShapeDtypeStruct(block, left.dtype),
            jax.ShapeDtypeStruct((GROUPS, chips * depth), jnp.int32),
        ),
        in_specs=[scalar] + [outside] * 5,
        out_specs=[inside] * 5,
        scratch_shapes=[
            pltpu.SMEM(rank.shape, jnp.int32),
            pltpu.SMEM(lag.shape, jnp.int32),
            pltpu.VMEM((GROUPS, *block), right.dtype),
            pltpu.VMEM((GROUPS, *block), left.dtype),
            semaphores((3,)),
            semaphores((GROUPS + 1,)),
            semaphores((GROUPS + 1,)),
        ],
        compiler_params=pltpu.CompilerParams(vmem_limit_bytes=16 << 20),
        cost_estimate=cost,
        name="far_away",
    )(core, rank, lag, history, right, left)

    def own():
        return pl.pallas_call(
            own_kernel,
            out_shape=field,
            in_specs=[scalar] + [inside] * 4 + [outside] * 2,
            out_specs=inside,
            scratch_shapes=[
                pltpu.VMEM((GROUPS - 1, *block), right.dtype),
                pltpu.VMEM((GROUPS - 1, *block), left.dtype),
                semaphores((GROUPS - 1,)),
                semaphores((GROUPS - 1,)),
            ],
            compiler_params=pltpu.CompilerParams(vmem_limit_bytes=16 << 20),
            cost_estimate=cost,
            name="far_own",
        )(core, hist_buf, right_own, left_own, columns, right, left)

    return away, own


def halves_kernel(mine_ref, came_ref, out_ref, held_ref, sem):
    copies = []
    for piece in range(mine_ref.shape[0]):
        held_ref[piece] = mine_ref[piece] + came_ref[piece]
        copies.append(
            pltpu.make_async_copy(held_ref.at[piece], out_ref.at[piece], sem.at[piece])
        )
        copies[-1].start()
    for copy in copies:
        copy.wait()


def halves_sum(mine, came):
    inside = pl.BlockSpec(memory_space=pltpu.VMEM)
    return pl.pallas_call(
        halves_kernel,
        out_shape=jax.ShapeDtypeStruct(mine.shape, mine.dtype),
        in_specs=[inside, inside],
        out_specs=pl.BlockSpec(memory_space=pltpu.HBM),
        scratch_shapes=[
            pltpu.VMEM(mine.shape, mine.dtype),
            pltpu.SemaphoreType.DMA((mine.shape[0],)),
        ],
        compiler_params=pltpu.CompilerParams(vmem_limit_bytes=4 << 20),
        cost_estimate=pl.CostEstimate(
            flops=mine.size, bytes_accessed=6 * mine.size, transcendentals=0
        ),
        name="halves_sum",
    )(mine, came)


def plane_kernel(in_ref, out_ref, held_ref, sem):
    copies = []
    pieces, rows, _ = held_ref.shape
    for piece in range(pieces):
        part = slice(piece * rows, (piece + 1) * rows)
        total = in_ref[0, part].astype(jnp.float32)
        for source in range(1, in_ref.shape[0]):
            total = total + in_ref[source, part].astype(jnp.float32)
        held_ref[piece] = total.astype(held_ref.dtype)
        for twin in range(out_ref.shape[0]):
            copies.append(
                pltpu.make_async_copy(
                    held_ref.at[piece], out_ref.at[twin, part], sem.at[twin, piece]
                )
            )
            copies[-1].start()
    for copy in copies:
        copy.wait()


def plane_sum(arrived, copies):
    pieces = 4
    return pl.pallas_call(
        plane_kernel,
        out_shape=jax.ShapeDtypeStruct((copies, *arrived.shape[1:]), arrived.dtype),
        in_specs=[pl.BlockSpec(memory_space=pltpu.VMEM)],
        out_specs=pl.BlockSpec(memory_space=pltpu.HBM),
        scratch_shapes=[
            pltpu.VMEM((pieces, arrived.shape[1] // pieces, arrived.shape[2]), arrived.dtype),
            pltpu.SemaphoreType.DMA((copies, pieces)),
        ],
        compiler_params=pltpu.CompilerParams(vmem_limit_bytes=4 << 20),
        cost_estimate=pl.CostEstimate(
            flops=arrived.size, bytes_accessed=2 * arrived.size, transcendentals=0
        ),
        name="plane_sum",
    )(arrived)


def last_kernel(
    where_ref, own_ref, second_ref, first_ref, third_ref, incoming_ref, shifted_ref,
    out_ref, next_ref, front_ref, out_sem, next_sem
):
    row = where_ref[0]
    rows = own_ref.shape[0]
    copies = []
    for turn, piece in enumerate((own_ref, first_ref, second_ref, third_ref)):
        at = pl.ds(pl.multiple_of(lax.rem(row + 4 - turn, 4) * rows, rows), rows)
        copies.append(pltpu.make_async_copy(piece, out_ref.at[at], out_sem.at[turn]))
        copies[-1].start()
        front_ref[at] = piece[...].astype(front_ref.dtype)
    front_ref[...] = jnp.where(where_ref[1] == 1, front_ref[...], incoming_ref[...])
    copies.append(pltpu.make_async_copy(front_ref, next_ref.at[0], next_sem))
    copies[-1].start()
    for copy in copies:
        copy.wait()


def finish(where, pieces, incoming, shifted):
    steps, width = incoming.shape
    inside, outside = (pl.BlockSpec(memory_space=m) for m in (pltpu.VMEM, pltpu.HBM))
    return pl.pallas_call(
        last_kernel,
        out_shape=(
            jax.ShapeDtypeStruct((steps, width), jnp.float32),
            jax.ShapeDtypeStruct(shifted.shape, shifted.dtype),
        ),
        in_specs=[pl.BlockSpec(memory_space=pltpu.SMEM)] + [inside] * 5 + [outside],
        out_specs=(outside, outside),
        scratch_shapes=[
            pltpu.VMEM((steps, width), jnp.bfloat16),
            pltpu.SemaphoreType.DMA((4,)),
            pltpu.SemaphoreType.DMA,
        ],
        input_output_aliases={6: 1},
        compiler_params=pltpu.CompilerParams(vmem_limit_bytes=4 << 20),
        name="finish",
    )(where, *pieces, incoming, shifted)


def times(value, block_ref):
    return lax.dot_general(
        value, block_ref, (((1,), (1,)), ((), ())), preferred_element_type=jnp.float32
    )


def right_kernel(arrived_ref, given_ref, inv_ref, c_ref, value_ref):
    total = arrived_ref[0].astype(jnp.float32)
    for source in range(1, arrived_ref.shape[0]):
        total = total + arrived_ref[source].astype(jnp.float32)
    c = given_ref[...] - inv_ref[...] * total
    c_ref[...] = c
    value_ref[...] = c.astype(jnp.bfloat16)


def inner_kernel(value_ref, beside_ref, c_ref, inv_ref, own_ref, chip_ref, part_ref):
    beside = beside_ref[...].astype(jnp.bfloat16)
    total = times(value_ref[...], own_ref[...]) + times(beside, chip_ref[...])
    part_ref[...] = c_ref[...] - inv_ref[...] * total


def simple_kernel(part_ref, got_ref, inv_ref, away_ref, value_ref):
    value = part_ref[...] - inv_ref[...] * times(got_ref[...], away_ref[...])
    value_ref[...] = value.astype(jnp.bfloat16)


def one_kernel(value_ref, c_ref, inv_ref, own_ref, part_ref):
    part_ref[...] = c_ref[...] - inv_ref[...] * times(value_ref[...], own_ref[...])


def begin_kernel(value_ref, part_ref, beside_ref, inv_ref, chip_ref, pack_ref, p_ref):
    part = part_ref[...] - inv_ref[...] * times(beside_ref[...], chip_ref[...])
    pack_ref[0] = value_ref[...]
    pack_ref[1] = part.astype(jnp.bfloat16)
    p_ref[...] = part


def ahead_kernel(pack_ref, back_ref, out_ref):
    out_ref[...] = times(pack_ref[0], back_ref[...])


def first_kernel(known_ref, p_ref, got_ref, inv_ref, away_ref, next_ref):
    mine = p_ref[...] - inv_ref[...] * times(got_ref[0], away_ref[...])
    other = got_ref[1].astype(jnp.float32) - known_ref[...]
    next_ref[0] = mine.astype(jnp.bfloat16)
    next_ref[1] = other.astype(jnp.bfloat16)


def under_kernel(
    next_ref, c_ref, c_u_ref, inv_ref, inv_u_ref, own_ref, away_ref, chip_u_ref, part_ref, part_u_ref
):
    total = times(next_ref[0], own_ref[...]) + times(next_ref[1], away_ref[...])
    part_ref[...] = c_ref[...] - inv_ref[...] * total
    part_u_ref[...] = c_u_ref[...] - inv_u_ref[...] * times(next_ref[0], chip_u_ref[...])


def second_kernel(
    got_ref, part_ref, part_u_ref, c_ref, inv_ref, inv_u_ref, own_ref, chip_ref, own_u_ref,
    away_u_ref, pack_ref, p_ref
):
    value = part_ref[...] - inv_ref[...] * times(got_ref[0], chip_ref[...])
    total_u = times(got_ref[0], own_u_ref[...]) + times(got_ref[1], away_u_ref[...])
    value = value.astype(jnp.bfloat16)
    beside = (part_u_ref[...] - inv_u_ref[...] * total_u).astype(jnp.bfloat16)
    part = c_ref[...] - inv_ref[...] * (times(value, own_ref[...]) + times(beside, chip_ref[...]))
    pack_ref[0] = value
    pack_ref[1] = part.astype(jnp.bfloat16)
    p_ref[...] = part


def last_under_kernel(next_ref, c_ref, inv_ref, own_ref, away_ref, part_ref):
    total = times(next_ref[0], own_ref[...]) + times(next_ref[1], away_ref[...])
    part_ref[...] = c_ref[...] - inv_ref[...] * total


def end_kernel(part_ref, got_ref, inv_ref, chip_ref, out_ref):
    out_ref[...] = part_ref[...] - inv_ref[...] * times(got_ref[0], chip_ref[...])


def small_call(kernel, products, outs, *operands):
    inside = pl.BlockSpec(memory_space=pltpu.VMEM)
    rows, width = outs[0].shape[-2:]
    return pl.pallas_call(
        kernel,
        out_shape=outs,
        in_specs=[inside] * len(operands),
        out_specs=[inside] * len(outs),
        compiler_params=pltpu.CompilerParams(vmem_limit_bytes=8 << 20),
        cost_estimate=pl.CostEstimate(
            flops=2 * products * rows * width * width,
            bytes_accessed=2 * products * width * width,
            transcendentals=0,
        ),
    )(*operands)


def per_device(
    history, right_factor, left_factor, pair_rank, pair_lag, near_block, self_term, excitation
):
    _, time_steps, width = history.shape
    pairs, ranks, _ = right_factor.shape
    targets = 32
    depth = pairs // targets * ranks
    right = right_factor.reshape(targets // 2, 2, depth, width)
    left = left_factor.reshape(targets // 2, 2, depth, width)
    history_out, right, left, rank, lag = (
        pltpu.with_memory_space_constraint(v, pltpu.HBM)
        for v in (history, right, left, pair_rank[:, 0], pair_lag[:, 0])
    )
    core = lax.axis_index("c")
    swap = [(0, 1), (1, 0)]

    away, own_half = far_halves(core.reshape(1), rank, lag, history_out, right, left, ranks)
    came = lax.ppermute(away, "c", swap)
    mine = own_half()
    partial_value = halves_sum(mine, came)
    arrived = lax.all_to_all(partial_value.reshape(16, -1, width), ("x", "y"), 0, 0, tiled=True)
    incoming = lax.ppermute(history[-1], HIST, [(i, (i + 1) % 8) for i in range(8)])
    near_u = lax.ppermute(near_block, "c", swap)
    self_u = lax.ppermute(self_term[None, :], "c", swap)

    block = lax.axis_index(SPACE)
    inverse, inverse_u = 1.0 / self_term[None, :], 1.0 / self_u

    def sides(blocks, even, at):
        chip = jnp.where(even, blocks[2], blocks[0])
        away = jnp.where(even, blocks[0], blocks[2])
        away = jnp.where((at == 0) | (at == targets - 1), 0.0, away)
        return chip, away

    near_own = near_block[1]
    near_chip, near_away = sides(near_block, core == 0, block)
    toward = (inverse.reshape(width, 1) * near_away).astype(jnp.bfloat16)
    rows = time_steps // 4
    row = lax.axis_index("y")
    given = lax.dynamic_slice_in_dim(excitation, row * rows, rows, 0) * inverse
    (
        arrived, incoming, near_u, inverse_u, near_chip, near_away, toward, given
    ) = lax.optimization_barrier(
        (arrived, incoming, near_u, inverse_u, near_chip, near_away, toward, given)
    )
    chip_u, away_u = sides(near_u, core == 1, block + 1 - 2 * core)
    own_u = near_u[1]
    shifted = jnp.concatenate([incoming[None], history[:-1]], axis=0)
    partner = {0: 0, targets - 1: targets - 1}
    for t in range(1, targets - 1, 2):
        partner[t], partner[t + 1] = t + 1, t
    between = []
    for t, other in partner.items():
        for y in range(4):
            between.append((t * 4 + y, other * 4 + (y ^ 1 if other == t else y)))

    def off_chip(value):
        return lax.ppermute(value, SPACE + ("y",), between)

    twice = plane_sum(arrived, 2).reshape(8, -1, width)
    arrived = lax.all_to_all(twice, ("zh", "zl"), 0, 0, tiled=True)
    back = off_chip(toward)
    back = jnp.where((block == 0) | (block == targets - 1), 0.0, back)
    arrived, incoming, shifted, chip_u, away_u = lax.optimization_barrier(
        (arrived, incoming, shifted, chip_u, away_u)
    )
    packed = jax.ShapeDtypeStruct((2, rows, width), jnp.bfloat16)
    single = jax.ShapeDtypeStruct((rows, width), jnp.float32)
    rounded = jax.ShapeDtypeStruct((rows, width), jnp.bfloat16)
    c, value = small_call(right_kernel, 0, (single, rounded), arrived, given, inverse)
    got = off_chip(value)
    c_u = lax.ppermute(c, "c", swap)
    (part,) = small_call(inner_kernel, 2, (single,), value, c_u, c, inverse, near_own, near_chip)
    (value,) = small_call(simple_kernel, 1, (rounded,), part, got, inverse, near_away)
    beside = lax.ppermute(value, "c", swap)
    (part,) = small_call(one_kernel, 1, (single,), value, c, inverse, near_own)
    pack, part = small_call(
        begin_kernel, 1, (packed, single), value, part, beside, inverse, near_chip
    )
    for sweep in range(2, SWEEPS, 2):
        got = off_chip(pack)
        (known,) = small_call(ahead_kernel, 1, (single,), pack, back)
        (both,) = small_call(first_kernel, 1, (packed,), known, part, got, inverse, near_away)
        over = lax.ppermute(both, "c", swap)
        if sweep + 2 >= SWEEPS:
            (part,) = small_call(
                last_under_kernel, 2, (single,),
                both, c, inverse, near_own, near_away,
            )
            (current,) = small_call(end_kernel, 1, (single,), part, over, inverse, near_chip)
            break
        part, part_u = small_call(
            under_kernel, 3, (single, single),
            both, c, c_u, inverse, inverse_u, near_own, near_away, chip_u,
        )
        pack, part = small_call(
            second_kernel, 5, (packed, single),
            over, part, part_u, c, inverse, inverse_u, near_own, near_chip, own_u, away_u,
        )

    pieces = [current]
    for step in (2, 1, 3):
        pieces.append(
            lax.ppermute(current, "y", [(i, (i + step) % 4) for i in range(4)])
        )
    oldest = ((lax.axis_index("zh") == 0) & (row == 0)).astype(jnp.int32)
    return finish(jnp.stack([row, oldest]), pieces, incoming, shifted)


def solution(mesh):
    fine = Mesh(mesh.devices.reshape(4, 4, 2, 2, 4), SPACE + HIST)
    in_specs = (
        P(HIST, None, SPACE),
        P(HIST, None, SPACE),
        P(HIST, None, SPACE),
        P(HIST, SPACE),
        P(HIST, SPACE),
        P(None, SPACE, None),
        P(SPACE),
        P(None, SPACE),
    )
    out_specs = (P(None, SPACE), P(HIST, None, SPACE))
    return jax.shard_map(
        per_device, mesh=fine, in_specs=in_specs, out_specs=out_specs, check_vma=False
    )
```

```python
import functools

import jax
import jax.numpy as jnp
from jax import lax
from jax.experimental import pallas as pl
from jax.experimental.pallas import tpu as pltpu
from jax.sharding import Mesh
from jax.sharding import PartitionSpec as P


SWEEPS = 8
SPACE = ("zl", "x", "c")
HIST = ("zh", "y")


GROUPS = 2


def brought(source, target, sem, group, core):
    chips = target.shape[0]
    return pltpu.make_async_copy(source.at[pl.ds(group * chips, chips), core], target, sem)


def column_of(group, core, rank_ref, lag_ref, chips, depth, ranks):
    lane = lax.broadcasted_iota(jnp.int32, (1, chips * depth), 1)
    column = jnp.full((1, chips * depth), -1, jnp.int32)
    per = depth // ranks
    for chip in range(chips):
        for k in range(per):
            pair = ((group * chips + chip) * 2 + core) * per + k
            first = (chip * per + k) * ranks
            inside = (lane >= first) & (lane < first + rank_ref[pair])
            column = jnp.where(inside, lag_ref[pair], column)
    return column


def chosen(hist_ref, right_ref, column):
    lags, steps, width = hist_ref.shape
    every = lax.dot_general(
        hist_ref[...].reshape(lags * steps, width),
        right_ref[...].reshape(-1, width),
        (((1,), (1,)), ((), ())),
        preferred_element_type=jnp.float32,
    )
    value = jnp.zeros((steps, every.shape[1]), jnp.float32)
    for lag in range(lags):
        value = jnp.where(column == lag, every[lag * steps : (lag + 1) * steps], value)
    return value.astype(jnp.bfloat16)


def far(group, value, left_ref, out_ref):
    chips, depth, width = left_ref.shape
    left = left_ref[...].reshape(chips * depth, width)
    for chip in range(chips):
        first, last = chip * depth, (chip + 1) * depth
        low, high = first // 128 * 128, -(-last // 128) * 128
        part = value[:, low:high]
        at = lax.broadcasted_iota(jnp.int32, part.shape, 1) + low
        part = jnp.where((at >= first) & (at < last), part, jnp.zeros_like(part))
        field = jnp.dot(part, left[low:high], preferred_element_type=jnp.float32)
        line = group * (chips // 4) + chip // 4
        out_ref[chip % 4, :, line] = field.reshape(out_ref.shape[1], -1, width).astype(out_ref.dtype)


def away_kernel(
    core_ref, rank_ref, lag_ref, hist_ref, right_ref, left_ref,
    out_ref, hist_buf, right_own, columns_ref,
    rank_buf, lag_buf, right_buf, left_buf, small_sem, right_sem, left_sem, *, ranks
):
    groups, chips, depth, _ = right_buf.shape
    core = core_ref[0]
    other = 1 - core
    small = [
        pltpu.make_async_copy(rank_ref, rank_buf, small_sem.at[0]),
        pltpu.make_async_copy(lag_ref, lag_buf, small_sem.at[1]),
        pltpu.make_async_copy(hist_ref, hist_buf, small_sem.at[2]),
    ]
    for copy in small:
        copy.start()
    rights = [
        brought(right_ref, right_buf.at[g], right_sem.at[g], g, other) for g in range(groups)
    ]
    lefts = [brought(left_ref, left_buf.at[g], left_sem.at[g], g, other) for g in range(groups)]
    for g in range(groups):
        rights[g].start()
        lefts[g].start()
    late = brought(right_ref, right_own, right_sem.at[groups], 0, core)
    late.start()
    small[0].wait()
    small[1].wait()
    columns = []
    for g in range(groups):
        columns.append(column_of(g, other, rank_buf, lag_buf, chips, depth, ranks))
        columns_ref[g : g + 1] = column_of(g, core, rank_buf, lag_buf, chips, depth, ranks)
    small[2].wait()
    rights[0].wait()
    value = chosen(hist_buf, right_buf.at[0], columns[0])
    for g in range(groups):
        lefts[g].wait()
        ahead = None
        if g + 1 < groups:
            rights[g + 1].wait()
            ahead = chosen(hist_buf, right_buf.at[g + 1], columns[g + 1])
        far(g, value, left_buf.at[g], out_ref)
        value = ahead
    late.wait()


def own_kernel(
    core_ref, hist_ref, right_own, columns_ref, right_ref, left_ref, out_ref,
    right_buf, left_buf, right_sem, left_sem
):
    core = core_ref[0]
    groups = left_buf.shape[0]
    lefts = [brought(left_ref, left_buf.at[g], left_sem.at[g], g, core) for g in range(groups)]
    rights = [
        brought(right_ref, right_buf.at[g], right_sem.at[g], g + 1, core) for g in range(groups - 1)
    ]
    for g in range(groups):
        lefts[g].start()
        if g + 1 < groups:
            rights[g].start()
    value = chosen(hist_ref, right_own, columns_ref[0:1])
    for g in range(groups):
        lefts[g].wait()
        ahead = None
        if g + 1 < groups:
            rights[g].wait()
            ahead = chosen(hist_ref, right_buf.at[g], columns_ref[g + 1 : g + 2])
        far(g, value, left_buf.at[g], out_ref)
        value = ahead


def far_halves(core, rank, lag, history, right, left, ranks):
    rows, _, depth, width = right.shape
    lags, steps, _ = history.shape
    chips = rows // GROUPS
    field = jax.ShapeDtypeStruct((4, 4, 4, steps // 4, width), jnp.bfloat16)
    block = (chips, depth, width)
    scalar = pl.BlockSpec(memory_space=pltpu.SMEM)
    inside = pl.BlockSpec(memory_space=pltpu.VMEM)
    outside = pl.BlockSpec(memory_space=pltpu.HBM)
    cost = pl.CostEstimate(
        flops=2 * rows * depth * width * (lags + 1) * steps,
        bytes_accessed=rows * depth * width * 4 + rows * steps * width * 2,
        transcendentals=0,
    )
    semaphores = pltpu.SemaphoreType.DMA
    away, hist_buf, right_own, columns = pl.pallas_call(
        functools.partial(away_kernel, ranks=ranks),
        out_shape=(
            field,
            jax.ShapeDtypeStruct(history.shape, history.dtype),
            jax.ShapeDtypeStruct(block, right.dtype),
            jax.ShapeDtypeStruct((GROUPS, chips * depth), jnp.int32),
        ),
        in_specs=[scalar] + [outside] * 5,
        out_specs=[inside] * 4,
        scratch_shapes=[
            pltpu.SMEM(rank.shape, jnp.int32),
            pltpu.SMEM(lag.shape, jnp.int32),
            pltpu.VMEM((GROUPS, *block), right.dtype),
            pltpu.VMEM((GROUPS, *block), left.dtype),
            semaphores((3,)),
            semaphores((GROUPS + 1,)),
            semaphores((GROUPS,)),
        ],
        compiler_params=pltpu.CompilerParams(vmem_limit_bytes=16 << 20),
        cost_estimate=cost,
        name="far_away",
    )(core, rank, lag, history, right, left)

    def own():
        return pl.pallas_call(
            own_kernel,
            out_shape=field,
            in_specs=[scalar] + [inside] * 3 + [outside] * 2,
            out_specs=inside,
            scratch_shapes=[
                pltpu.VMEM((GROUPS - 1, *block), right.dtype),
                pltpu.VMEM((GROUPS, *block), left.dtype),
                semaphores((GROUPS - 1,)),
                semaphores((GROUPS,)),
            ],
            compiler_params=pltpu.CompilerParams(vmem_limit_bytes=16 << 20),
            cost_estimate=cost,
            name="far_own",
        )(core, hist_buf, right_own, columns, right, left)

    return away, own


def halves_kernel(mine_ref, came_ref, out_ref, held_ref, sem):
    copies = []
    for piece in range(mine_ref.shape[0]):
        held_ref[piece] = mine_ref[piece] + came_ref[piece]
        copies.append(
            pltpu.make_async_copy(held_ref.at[piece], out_ref.at[piece], sem.at[piece])
        )
        copies[-1].start()
    for copy in copies:
        copy.wait()


def halves_sum(mine, came):
    inside = pl.BlockSpec(memory_space=pltpu.VMEM)
    return pl.pallas_call(
        halves_kernel,
        out_shape=jax.ShapeDtypeStruct(mine.shape, mine.dtype),
        in_specs=[inside, inside],
        out_specs=pl.BlockSpec(memory_space=pltpu.HBM),
        scratch_shapes=[
            pltpu.VMEM(mine.shape, mine.dtype),
            pltpu.SemaphoreType.DMA((mine.shape[0],)),
        ],
        compiler_params=pltpu.CompilerParams(vmem_limit_bytes=4 << 20),
        cost_estimate=pl.CostEstimate(
            flops=mine.size, bytes_accessed=6 * mine.size, transcendentals=0
        ),
        name="halves_sum",
    )(mine, came)


def plane_kernel(in_ref, out_ref, held_ref, sem):
    copies = []
    pieces, rows, _ = held_ref.shape
    for piece in range(pieces):
        part = slice(piece * rows, (piece + 1) * rows)
        total = in_ref[0, part].astype(jnp.float32)
        for source in range(1, in_ref.shape[0]):
            total = total + in_ref[source, part].astype(jnp.float32)
        held_ref[piece] = total.astype(held_ref.dtype)
        for twin in range(out_ref.shape[0]):
            copies.append(
                pltpu.make_async_copy(
                    held_ref.at[piece], out_ref.at[twin, part], sem.at[twin, piece]
                )
            )
            copies[-1].start()
    for copy in copies:
        copy.wait()


def plane_sum(arrived, copies):
    pieces = 4
    return pl.pallas_call(
        plane_kernel,
        out_shape=jax.ShapeDtypeStruct((copies, *arrived.shape[1:]), arrived.dtype),
        in_specs=[pl.BlockSpec(memory_space=pltpu.VMEM)],
        out_specs=pl.BlockSpec(memory_space=pltpu.HBM),
        scratch_shapes=[
            pltpu.VMEM((pieces, arrived.shape[1] // pieces, arrived.shape[2]), arrived.dtype),
            pltpu.SemaphoreType.DMA((copies, pieces)),
        ],
        compiler_params=pltpu.CompilerParams(vmem_limit_bytes=4 << 20),
        cost_estimate=pl.CostEstimate(
            flops=arrived.size, bytes_accessed=2 * arrived.size, transcendentals=0
        ),
        name="plane_sum",
    )(arrived)


def last_kernel(
    where_ref, own_ref, second_ref, first_ref, third_ref, incoming_ref, shifted_ref,
    out_ref, next_ref, front_ref, out_sem, next_sem
):
    row = where_ref[0]
    rows = own_ref.shape[0]
    copies = []
    for turn, piece in enumerate((own_ref, first_ref, second_ref, third_ref)):
        at = pl.ds(pl.multiple_of(lax.rem(row + 4 - turn, 4) * rows, rows), rows)
        copies.append(pltpu.make_async_copy(piece, out_ref.at[at], out_sem.at[turn]))
        copies[-1].start()
        front_ref[at] = piece[...].astype(front_ref.dtype)
    front_ref[...] = jnp.where(where_ref[1] == 1, front_ref[...], incoming_ref[...])
    copies.append(pltpu.make_async_copy(front_ref, next_ref.at[0], next_sem))
    copies[-1].start()
    for copy in copies:
        copy.wait()


def finish(where, pieces, incoming, shifted):
    steps, width = incoming.shape
    inside, outside = (pl.BlockSpec(memory_space=m) for m in (pltpu.VMEM, pltpu.HBM))
    return pl.pallas_call(
        last_kernel,
        out_shape=(
            jax.ShapeDtypeStruct((steps, width), jnp.float32),
            jax.ShapeDtypeStruct(shifted.shape, shifted.dtype),
        ),
        in_specs=[pl.BlockSpec(memory_space=pltpu.SMEM)] + [inside] * 5 + [outside],
        out_specs=(outside, outside),
        scratch_shapes=[
            pltpu.VMEM((steps, width), jnp.bfloat16),
            pltpu.SemaphoreType.DMA((4,)),
            pltpu.SemaphoreType.DMA,
        ],
        input_output_aliases={6: 1},
        compiler_params=pltpu.CompilerParams(vmem_limit_bytes=4 << 20),
        name="finish",
    )(where, *pieces, incoming, shifted)


def times(value, block_ref):
    return lax.dot_general(
        value, block_ref, (((1,), (1,)), ((), ())), preferred_element_type=jnp.float32
    )


def right_kernel(arrived_ref, given_ref, inv_ref, c_ref, value_ref):
    total = arrived_ref[0].astype(jnp.float32)
    for source in range(1, arrived_ref.shape[0]):
        total = total + arrived_ref[source].astype(jnp.float32)
    c = given_ref[...] - inv_ref[...] * total
    c_ref[...] = c
    value_ref[...] = c.astype(jnp.bfloat16)


def inner_kernel(value_ref, beside_ref, c_ref, inv_ref, own_ref, chip_ref, part_ref):
    beside = beside_ref[...].astype(jnp.bfloat16)
    total = times(value_ref[...], own_ref[...]) + times(beside, chip_ref[...])
    part_ref[...] = c_ref[...] - inv_ref[...] * total


def simple_kernel(part_ref, got_ref, inv_ref, away_ref, value_ref):
    value = part_ref[...] - inv_ref[...] * times(got_ref[...], away_ref[...])
    value_ref[...] = value.astype(jnp.bfloat16)


def one_kernel(value_ref, c_ref, inv_ref, own_ref, part_ref):
    part_ref[...] = c_ref[...] - inv_ref[...] * times(value_ref[...], own_ref[...])


def begin_kernel(value_ref, part_ref, beside_ref, inv_ref, chip_ref, pack_ref, p_ref):
    part = part_ref[...] - inv_ref[...] * times(beside_ref[...], chip_ref[...])
    pack_ref[0] = value_ref[...]
    pack_ref[1] = part.astype(jnp.bfloat16)
    p_ref[...] = part


def ahead_kernel(pack_ref, back_ref, out_ref):
    out_ref[...] = times(pack_ref[0], back_ref[...])


def first_kernel(known_ref, p_ref, got_ref, inv_ref, away_ref, next_ref):
    mine = p_ref[...] - inv_ref[...] * times(got_ref[0], away_ref[...])
    other = got_ref[1].astype(jnp.float32) - known_ref[...]
    next_ref[0] = mine.astype(jnp.bfloat16)
    next_ref[1] = other.astype(jnp.bfloat16)


def under_kernel(
    next_ref, c_ref, c_u_ref, inv_ref, inv_u_ref, own_ref, away_ref, chip_u_ref, part_ref, part_u_ref
):
    total = times(next_ref[0], own_ref[...]) + times(next_ref[1], away_ref[...])
    part_ref[...] = c_ref[...] - inv_ref[...] * total
    part_u_ref[...] = c_u_ref[...] - inv_u_ref[...] * times(next_ref[0], chip_u_ref[...])


def second_kernel(
    got_ref, part_ref, part_u_ref, c_ref, inv_ref, inv_u_ref, own_ref, chip_ref, own_u_ref,
    away_u_ref, pack_ref, p_ref
):
    value = part_ref[...] - inv_ref[...] * times(got_ref[0], chip_ref[...])
    total_u = times(got_ref[0], own_u_ref[...]) + times(got_ref[1], away_u_ref[...])
    value = value.astype(jnp.bfloat16)
    beside = (part_u_ref[...] - inv_u_ref[...] * total_u).astype(jnp.bfloat16)
    part = c_ref[...] - inv_ref[...] * (times(value, own_ref[...]) + times(beside, chip_ref[...]))
    pack_ref[0] = value
    pack_ref[1] = part.astype(jnp.bfloat16)
    p_ref[...] = part


def last_under_kernel(next_ref, c_ref, inv_ref, own_ref, away_ref, part_ref):
    total = times(next_ref[0], own_ref[...]) + times(next_ref[1], away_ref[...])
    part_ref[...] = c_ref[...] - inv_ref[...] * total


def end_kernel(part_ref, got_ref, inv_ref, chip_ref, out_ref):
    out_ref[...] = part_ref[...] - inv_ref[...] * times(got_ref[0], chip_ref[...])


def small_call(kernel, products, outs, *operands):
    inside = pl.BlockSpec(memory_space=pltpu.VMEM)
    rows, width = outs[0].shape[-2:]
    return pl.pallas_call(
        kernel,
        out_shape=outs,
        in_specs=[inside] * len(operands),
        out_specs=[inside] * len(outs),
        compiler_params=pltpu.CompilerParams(vmem_limit_bytes=8 << 20),
        cost_estimate=pl.CostEstimate(
            flops=2 * products * rows * width * width,
            bytes_accessed=2 * products * width * width,
            transcendentals=0,
        ),
    )(*operands)


def per_device(
    history, right_factor, left_factor, pair_rank, pair_lag, near_block, self_term, excitation
):
    _, time_steps, width = history.shape
    pairs, ranks, _ = right_factor.shape
    targets = 32
    depth = pairs // targets * ranks
    right = right_factor.reshape(targets // 2, 2, depth, width)
    left = left_factor.reshape(targets // 2, 2, depth, width)
    history_out, right, left, rank, lag = (
        pltpu.with_memory_space_constraint(v, pltpu.HBM)
        for v in (history, right, left, pair_rank[:, 0], pair_lag[:, 0])
    )
    core = lax.axis_index("c")
    swap = [(0, 1), (1, 0)]

    away, own_half = far_halves(core.reshape(1), rank, lag, history_out, right, left, ranks)
    came = lax.ppermute(away, "c", swap)
    mine = own_half()
    partial_value = halves_sum(mine, came)
    arrived = lax.all_to_all(partial_value.reshape(16, -1, width), ("x", "y"), 0, 0, tiled=True)
    incoming = lax.ppermute(history[-1], HIST, [(i, (i + 1) % 8) for i in range(8)])
    near_u = lax.ppermute(near_block, "c", swap)
    self_u = lax.ppermute(self_term[None, :], "c", swap)

    block = lax.axis_index(SPACE)
    inverse, inverse_u = 1.0 / self_term[None, :], 1.0 / self_u

    def sides(blocks, even, at):
        chip = jnp.where(even, blocks[2], blocks[0])
        away = jnp.where(even, blocks[0], blocks[2])
        away = jnp.where((at == 0) | (at == targets - 1), 0.0, away)
        return chip, away

    near_own = near_block[1]
    near_chip, near_away = sides(near_block, core == 0, block)
    toward = (inverse.reshape(width, 1) * near_away).astype(jnp.bfloat16)
    rows = time_steps // 4
    row = lax.axis_index("y")
    given = lax.dynamic_slice_in_dim(excitation, row * rows, rows, 0) * inverse
    (
        arrived, incoming, near_u, inverse_u, near_chip, near_away, toward, given
    ) = lax.optimization_barrier(
        (arrived, incoming, near_u, inverse_u, near_chip, near_away, toward, given)
    )
    chip_u, away_u = sides(near_u, core == 1, block + 1 - 2 * core)
    own_u = near_u[1]
    shifted = jnp.concatenate([incoming[None], history[:-1]], axis=0)
    partner = {0: 0, targets - 1: targets - 1}
    for t in range(1, targets - 1, 2):
        partner[t], partner[t + 1] = t + 1, t
    between = []
    for t, other in partner.items():
        for y in range(4):
            between.append((t * 4 + y, other * 4 + (y ^ 1 if other == t else y)))

    def off_chip(value):
        return lax.ppermute(value, SPACE + ("y",), between)

    twice = plane_sum(arrived, 2).reshape(8, -1, width)
    arrived = lax.all_to_all(twice, ("zh", "zl"), 0, 0, tiled=True)
    arrived, incoming, shifted, chip_u, away_u = lax.optimization_barrier(
        (arrived, incoming, shifted, chip_u, away_u)
    )
    packed = jax.ShapeDtypeStruct((2, rows, width), jnp.bfloat16)
    single = jax.ShapeDtypeStruct((rows, width), jnp.float32)
    rounded = jax.ShapeDtypeStruct((rows, width), jnp.bfloat16)
    c, value = small_call(right_kernel, 0, (single, rounded), arrived, given, inverse)
    got = off_chip(value)
    c_u = lax.ppermute(c, "c", swap)
    back = off_chip(toward)
    back = jnp.where((block == 0) | (block == targets - 1), 0.0, back)
    (part,) = small_call(inner_kernel, 2, (single,), value, c_u, c, inverse, near_own, near_chip)
    (value,) = small_call(simple_kernel, 1, (rounded,), part, got, inverse, near_away)
    beside = lax.ppermute(value, "c", swap)
    (part,) = small_call(one_kernel, 1, (single,), value, c, inverse, near_own)
    pack, part = small_call(
        begin_kernel, 1, (packed, single), value, part, beside, inverse, near_chip
    )
    for sweep in range(2, SWEEPS, 2):
        got = off_chip(pack)
        (known,) = small_call(ahead_kernel, 1, (single,), pack, back)
        (both,) = small_call(first_kernel, 1, (packed,), known, part, got, inverse, near_away)
        over = lax.ppermute(both, "c", swap)
        if sweep + 2 >= SWEEPS:
            (part,) = small_call(
                last_under_kernel, 2, (single,),
                both, c, inverse, near_own, near_away,
            )
            (current,) = small_call(end_kernel, 1, (single,), part, over, inverse, near_chip)
            break
        part, part_u = small_call(
            under_kernel, 3, (single, single),
            both, c, c_u, inverse, inverse_u, near_own, near_away, chip_u,
        )
        pack, part = small_call(
            second_kernel, 5, (packed, single),
            over, part, part_u, c, inverse, inverse_u, near_own, near_chip, own_u, away_u,
        )

    pieces = [current]
    for step in (2, 1, 3):
        pieces.append(
            lax.ppermute(current, "y", [(i, (i + step) % 4) for i in range(4)])
        )
    oldest = ((lax.axis_index("zh") == 0) & (row == 0)).astype(jnp.int32)
    return finish(jnp.stack([row, oldest]), pieces, incoming, shifted)


def solution(mesh):
    fine = Mesh(mesh.devices.reshape(4, 4, 2, 2, 4), SPACE + HIST)
    in_specs = (
        P(HIST, None, SPACE),
        P(HIST, None, SPACE),
        P(HIST, None, SPACE),
        P(HIST, SPACE),
        P(HIST, SPACE),
        P(None, SPACE, None),
        P(SPACE),
        P(None, SPACE),
    )
    out_specs = (P(None, SPACE), P(HIST, None, SPACE))
    return jax.shard_map(
        per_device, mesh=fine, in_specs=in_specs, out_specs=out_specs, check_vma=False
    )
```
